128 devices in a mesh: section: 8 (over z, y_lo), tensor: 16 (over x, y_hi, core).
Axes of the slice: x: 4, y: 4 (y_hi: 2, y_lo: 2; y = y_hi * 2 + y_lo), z: 4, core: 2. Of those that a mesh axis runs over, the one named last changes fastest.
Arguments:
- tokens: bfloat16 [384, 6144], P('tensor', 'section'), may hold values from -6 to 6
- combine: float32 [384, 2], replicated, may hold values from 0.1 to 1
- expert_ids: int32 [384, 2], replicated, may hold values from 0 to 3, as said below
- expert_counts: int32 [4], replicated, may hold values from 0 to 384, as said below
- w_gate: bfloat16 [4, 6144, 16384], P(None, 'section', 'tensor'), may hold values from -0.078125 to 0.078125
- w_up: bfloat16 [4, 6144, 16384], P(None, 'section', 'tensor'), may hold values from -0.078125 to 0.078125
- w_down: bfloat16 [4, 16384, 6144], P(None, 'tensor', 'section'), may hold values from -0.046875 to 0.046875
- cotangent: bfloat16 [384, 6144], P('tensor', 'section'), may hold values from -6 to 6
Outputs:
- layer_out: bfloat16 [384, 6144], P('tensor', 'section')
- d_tokens: bfloat16 [384, 6144], P('tensor', 'section')
- d_down: bfloat16 [4, 16384, 6144], P(None, 'tensor', 'section')
The draws below stay inside these ranges and needn't reach their ends.
Inputs may be any that keep to these rules, and one draw needn't show every extreme that they name: `expert_ids`: each row names two different experts; one expert, drawn from the seed, is named by every row. expert_counts[e] is the number of entries of expert_ids equal to e.
All inputs are finite; a program needn't handle non-finite values.
Results may differ from the reference program's by a relative error of at most 0.0058.
Values may be sent and summed in bfloat16 or wider, within the bound.
A program may use at most 128 MiB of HBM per device.

```python
import jax
import jax.numpy as jnp
from jax import lax

D = 6144
FF = 16384
EXPERTS = 4
BLOCK = 128
TOKENS = 384


def assignments(key):
    base = jax.random.fold_in(key, 17)
    first_key, second_key, label_key = jax.random.split(base, 3)
    first_raw = jax.random.randint(first_key, (TOKENS,), 0, 2 * EXPERTS)
    first_code = jnp.where(first_raw >= EXPERTS, 0, first_raw)
    labels = jax.random.permutation(label_key, EXPERTS)
    first = labels[first_code]
    other = labels[(first_code * 0 + jax.random.randint(second_key, (TOKENS,), 1, EXPERTS)) % EXPERTS]
    second = jnp.where(first_code == 0, other, labels[0])
    return jnp.stack([first, second], 1).astype(jnp.int32)


def draw_expert_ids(key, part):
    return assignments(key)


def draw_expert_counts(key, part):
    chosen = assignments(key).reshape(-1)
    onehot = (chosen[:, None] == jnp.arange(EXPERTS)[None, :]).astype(jnp.int32)
    return jnp.sum(onehot, 0).astype(jnp.int32)


def shard_levels(rng, extent, cuts, least, largest):
    level = 1.0
    for axis_at, blocks in cuts:
        steps = jax.random.uniform(jax.random.fold_in(jax.random.fold_in(rng, 6), axis_at), (blocks,), jnp.float32, least / len(cuts), largest / len(cuts))
        level = level * jnp.repeat(jnp.exp(steps), extent[axis_at] // blocks).reshape((-1,) + (1,) * (len(extent) - 1 - axis_at))
    return level


def noise(rng, extent, width, limit, cuts=(), kind=jnp.bfloat16):
    gain = shard_levels(rng, extent, cuts, -0.22, 0.18) if cuts else 1.0
    values = jax.random.normal(rng, extent, jnp.float32) * width * gain
    return jnp.minimum(jnp.maximum(values, -limit), limit).astype(kind)


def setup_inputs(seed: int = 0) -> dict:
    keys = jax.random.split(jax.random.key(seed), 9)
    tokens = noise(keys[0], (TOKENS, D), 1.0, 6.0, ((0, 16), (1, 8)))
    combine = jnp.clip(jax.random.uniform(keys[1], (TOKENS, 2), jnp.float32, 0.1, 1.0), 0.1, 1.0)
    expert_ids = draw_expert_ids(jax.random.fold_in(keys[8], 71), 0)
    expert_counts = draw_expert_counts(jax.random.fold_in(keys[8], 71), 0)
    w_gate = noise(keys[4], (EXPERTS, D, FF), D ** -0.5, 0.078125, ((1, 8), (2, 16)))
    w_up = noise(keys[5], (EXPERTS, D, FF), D ** -0.5, 0.078125, ((1, 8), (2, 16)))
    w_down = noise(keys[6], (EXPERTS, FF, D), FF ** -0.5, 0.046875, ((1, 16), (2, 8)))
    cotangent = noise(keys[7], (TOKENS, D), 1.0, 6.0, ((0, 16), (1, 8)))
    return dict(tokens=tokens, combine=combine, expert_ids=expert_ids, expert_counts=expert_counts, w_gate=w_gate, w_up=w_up, w_down=w_down, cotangent=cotangent)


def route_layout(expert_ids, expert_counts, tokens_total, capacity):
    flat_ids = expert_ids.reshape(-1).astype(jnp.int32)
    onehot = (flat_ids[:, None] == jnp.arange(EXPERTS, dtype=jnp.int32)[None, :]).astype(jnp.int32)
    within = jnp.sum((jnp.cumsum(onehot, 0) - onehot) * onehot, 1)
    padded = (expert_counts.astype(jnp.int32) + BLOCK - 1) // BLOCK * BLOCK
    block_ends = jnp.cumsum(padded)
    block_starts = block_ends - padded
    slot_index = jnp.sum(onehot * block_starts[None, :], 1) + within
    entry_token = jnp.arange(flat_ids.shape[0], dtype=jnp.int32) // 2
    owner_token = jnp.full((capacity,), tokens_total, jnp.int32).at[slot_index].set(entry_token)
    first_rows = jnp.arange(capacity // BLOCK, dtype=jnp.int32) * BLOCK
    block_expert = jnp.minimum(jnp.sum((block_ends[None, :] <= first_rows[:, None]).astype(jnp.int32), 1), EXPERTS - 1)
    return slot_index, owner_token, block_expert


def blocked_product(rows, weights, block_expert, transpose):
    nblocks = block_expert.shape[0]
    blocks = rows.reshape(nblocks, rows.shape[0] // nblocks, rows.shape[1])

    def apply_block(operand):
        segment, expert = operand
        matrix = lax.dynamic_index_in_dim(weights, expert, 0, keepdims=False)
        if transpose:
            return lax.dot_general(segment, matrix, (((1,), (1,)), ((), ())), preferred_element_type=jnp.float32)
        return jnp.dot(segment, matrix, preferred_element_type=jnp.float32)

    result = lax.map(apply_block, (blocks, block_expert))
    return result.reshape(rows.shape[0], result.shape[2])


def reference(tokens, combine, expert_ids, expert_counts, w_gate, w_up, w_down, cotangent):
    tokens_total = tokens.shape[0]
    capacity = 2 * tokens_total + EXPERTS * BLOCK
    slot_index, owner_token, block_expert = route_layout(expert_ids, expert_counts, tokens_total, capacity)
    slot_pairs = slot_index.reshape(tokens_total, 2)
    zero_row = jnp.zeros((1, tokens.shape[1]), tokens.dtype)
    rows = jnp.concatenate([tokens, zero_row], 0)[owner_token]
    gate = blocked_product(rows, w_gate, block_expert, False)
    up = blocked_product(rows, w_up, block_expert, False)
    sigmoid = jax.nn.sigmoid(gate)
    active = gate * sigmoid
    hidden = (active * up).astype(jnp.bfloat16)
    out_rows = blocked_product(hidden, w_down, block_expert, False)
    layer_out = jnp.sum(combine[:, :, None] * out_rows[slot_pairs], 1).astype(jnp.bfloat16)
    combine_slot = jnp.zeros((capacity,), jnp.float32).at[slot_index].set(combine.reshape(-1))
    cot_rows = jnp.concatenate([cotangent, zero_row], 0)[owner_token].astype(jnp.float32)
    row_grad = (combine_slot[:, None] * cot_rows).astype(jnp.bfloat16)
    d_hidden = blocked_product(row_grad, w_down, block_expert, True)
    row_expert = jnp.repeat(block_expert, BLOCK)
    grads = []
    for expert in range(EXPERTS):
        chosen = jnp.where((row_expert == expert)[:, None], hidden, jnp.zeros_like(hidden))
        grads.append(lax.dot_general(chosen, row_grad, (((0,), (0,)), ((), ())), preferred_element_type=jnp.float32).astype(jnp.bfloat16))
    d_down = jnp.stack(grads, 0)
    d_gate = (d_hidden * up * sigmoid * (1.0 + gate * (1.0 - sigmoid))).astype(jnp.bfloat16)
    d_up = (d_hidden * active).astype(jnp.bfloat16)
    d_rows = blocked_product(d_gate, w_gate, block_expert, True) + blocked_product(d_up, w_up, block_expert, True)
    d_tokens = jnp.sum(d_rows[slot_pairs], 1).astype(jnp.bfloat16)
    return layer_out, d_tokens, d_down
```

```python
import jax
import jax.numpy as jnp
from jax import lax
from jax.sharding import PartitionSpec as P

EXPERTS = 4


def on_device(tokens, combine, expert_ids, expert_counts, w_gate, w_up, w_down, cotangent):
    total = combine.shape[0]
    both = lax.all_gather(jnp.stack([tokens, cotangent]), "tensor", axis=1, tiled=True)
    x, cot = both[0], both[1].astype(jnp.float32)
    common = jnp.argmax(expert_counts == total).astype(jnp.int32)
    is_common = expert_ids == common
    comb_c = jnp.sum(jnp.where(is_common, combine, 0.0), 1)[:, None]
    comb_o = jnp.sum(jnp.where(is_common, 0.0, combine), 1)[:, None]
    other = jnp.sum(jnp.where(is_common, 0, expert_ids), 1)
    mask_o = [(other == e)[:, None] for e in range(EXPERTS)]
    rg_c = (comb_c * cot).astype(jnp.bfloat16)
    rg_o = (comb_o * cot).astype(jnp.bfloat16)

    def pick(rows):
        return jnp.concatenate([jnp.where(m, rows, jnp.zeros_like(rows)) for m in mask_o], 1)

    def dot(a, b, dims):
        return lax.dot_general(a, b, (dims, ((), ())), preferred_element_type=jnp.float32)

    d_loc, f_loc = w_gate.shape[1:]
    x_o = pick(x).reshape(total, EXPERTS, d_loc)
    g_o = pick(rg_o).reshape(total, EXPERTS, d_loc)
    take = lambda w: lax.dynamic_index_in_dim(w, common, 0, keepdims=False)
    gate_c = dot(x, take(w_gate), ((1,), (0,)))
    up_c = dot(x, take(w_up), ((1,), (0,)))
    dh_c = dot(rg_c, take(w_down), ((1,), (1,)))
    gate_o = dot(x_o, w_gate, ((1, 2), (0, 1)))
    up_o = dot(x_o, w_up, ((1, 2), (0, 1)))
    dh_o = dot(g_o, w_down, ((1, 2), (0, 2)))
    parts = jnp.stack([gate_c, gate_o, up_c, up_o, dh_c, dh_o]).astype(jnp.bfloat16)
    nsec = lax.axis_size("section")
    parts = parts.reshape(6, total, nsec, f_loc // nsec).transpose(2, 0, 1, 3)
    sums = lax.all_to_all(parts, "section", 0, 0, tiled=True).astype(jnp.float32).sum(0)
    gate, up, dh = sums[0:2], sums[2:4], sums[4:6]
    s = jax.nn.sigmoid(gate)
    act = gate * s
    mine = jnp.stack([act * up, dh * up * s * (1.0 + gate * (1.0 - s)), dh * act]).astype(jnp.bfloat16)
    full = lax.all_gather(mine, "section", axis=0)
    full = full.transpose(1, 2, 3, 0, 4).reshape(3, 2, total, f_loc)
    (h_c, h_o), (dg_c, dg_o), (du_c, du_o) = full[0], full[1], full[2]

    def pick_all(rows_c, rows_o):
        return [
            jnp.where(common == e, rows_c, jnp.where(mask_o[e], rows_o, jnp.zeros_like(rows_o)))
            for e in range(EXPERTS)
        ]

    hs, dgs, dus = pick_all(h_c, h_o), pick_all(dg_c, dg_o), pick_all(du_c, du_o)
    out = jnp.zeros((total, d_loc), jnp.float32)
    dtok = jnp.zeros((total, d_loc), jnp.float32)
    d_down = []
    for e in range(EXPERTS):
        comb_e = jnp.where(common == e, comb_c, comb_o)
        out += comb_e * dot(hs[e], w_down[e], ((1,), (0,)))
        dtok += dot(dgs[e], w_gate[e], ((1,), (1,))) + dot(dus[e], w_up[e], ((1,), (1,)))
        rg_e = jnp.where(common == e, rg_c, rg_o)
        d_down.append(dot(hs[e], rg_e, ((0,), (0,))).astype(jnp.bfloat16))
    res = lax.psum_scatter(jnp.stack([out, dtok]), "tensor", scatter_dimension=1, tiled=True)
    res = res.astype(jnp.bfloat16)
    return res[0], res[1], jnp.stack(d_down)


def solution(mesh):
    in_specs = (
        P("tensor", "section"),
        P(),
        P(),
        P(),
        P(None, "section", "tensor"),
        P(None, "section", "tensor"),
        P(None, "tensor", "section"),
        P("tensor", "section"),
    )
    out_specs = (P("tensor", "section"), P("tensor", "section"), P(None, "tensor", "section"))
    return jax.shard_map(
        on_device, mesh=mesh, in_specs=in_specs, out_specs=out_specs, check_vma=False
    )
```

```python
import jax
import jax.numpy as jnp
from jax import lax
from jax.experimental import pallas as pl
from jax.experimental.pallas import tpu as pltpu
from jax.sharding import PartitionSpec as P

EXPERTS = 4
NZ = 4
BF = jnp.bfloat16
F32 = jnp.float32
MESH = pl.DeviceIdType.MESH


def mm(a, b):
    return jnp.dot(a, b, preferred_element_type=F32)


def mm_nt(a, b):
    return lax.dot_general(a, b, (((1,), (1,)), ((), ())), preferred_element_type=F32)


def mm_tn(a, b):
    return lax.dot_general(a, b, (((0,), (0,)), ((), ())), preferred_element_type=F32)


def layer_kernel(
    c_ref, meta_ref, xt_ref, wg_hbm, wu_hbm, wd_hbm,
    lo_ref, dt_ref, dd_hbm,
    wgu, wd, xbuf, xf, cf, xs, xm, rgc, rgo, rgm, mo, cb,
    pa, paf, pb, pbf, rar, raf, sa, ray, rby, qb, rbr, rbf, hc, ho, dd, fs, fr, gs, gr,
    w_sem, loc_sem, x_send, x_recv, a_send, a_recv, b_send, b_recv,
    c_send, c_recv, o_send, o_recv, dd_sem, f_send, f_recv,
):
    tokens, dloc = xf.shape
    fc = pa.shape[-1]
    half = tokens // 2
    quart = half // 2
    bl = tokens // 16
    nt = dloc // 256

    s = lax.axis_index("section")
    t = lax.axis_index("tensor")
    z, yl = s // 2, s % 2
    zp = ((z + 1) % NZ) * 2 + yl
    zm = ((z + 3) % NZ) * 2 + yl
    yp = z * 2 + 1 - yl
    core, kt, x = t % 2, t // 2, t // 4
    yh = kt % 2

    def tx(d):
        return ((x + d) % 4) * 4 + yh * 2 + core

    ty = x * 4 + (1 - yh) * 2 + core
    sib = t + 1 - 2 * core

    def sec(src, dst, ssem, rsem, dev):
        return pltpu.make_async_remote_copy(src, dst, ssem, rsem, {"section": dev}, MESH)

    def ten(src, dst, ssem, rsem, dev):
        return pltpu.make_async_remote_copy(src, dst, ssem, rsem, {"tensor": dev}, MESH)

    for e in range(EXPERTS):
        pltpu.make_async_copy(wg_hbm.at[e], wgu.at[0, e], w_sem.at[0, e]).start()
        pltpu.make_async_copy(wu_hbm.at[e], wgu.at[1, e], w_sem.at[1, e]).start()
        pltpu.make_async_copy(wd_hbm.at[e], wd.at[e], w_sem.at[2, e]).start()

    barrier = pltpu.get_barrier_semaphore()
    for dev in (zp, zm, yp):
        pl.semaphore_signal(barrier, inc=1, device_id={"section": dev}, device_id_type=MESH)
    for k in range(1, 8):
        pl.semaphore_signal(
            barrier, inc=1, device_id={"tensor": ((kt + k) % 8) * 2 + core}, device_id_type=MESH
        )
    pl.semaphore_signal(barrier, inc=1, device_id={"tensor": sib}, device_id_type=MESH)
    pl.semaphore_wait(barrier, 11)

    q = core * 8 + kt
    qy = core * 8 + x * 2 + 1 - yh
    own_copy = pltpu.make_async_copy(xt_ref, xbuf.at[q], loc_sem)
    own_copy.start()
    targets = (ty, tx(1), tx(3), tx(2), sib)
    own_sends = [
        ten(xt_ref, xbuf.at[q], x_send.at[i], x_recv.at[q], dev) for i, dev in enumerate(targets)
    ]
    for cp in own_sends:
        cp.start()

    def x_wait(slot):
        ten(xt_ref, xbuf.at[slot], x_send.at[0], x_recv.at[slot], sib).wait_recv()

    x_wait(qy)
    fwd_sends = [
        ten(xbuf.at[qy], xbuf.at[qy], x_send.at[5 + i], x_recv.at[qy], dev)
        for i, dev in enumerate(targets[1:])
    ]
    for cp in fwd_sends:
        cp.start()
    n = 9
    for flip in (0, 1):
        for d in (1, 3, 2):
            other_y = yh + flip - 2 * yh * flip
            slot = core * 8 + ((x + d) % 4) * 2 + other_y
            x_wait(slot)
            cp = ten(xbuf.at[slot], xbuf.at[slot], x_send.at[n], x_recv.at[slot], sib)
            cp.start()
            fwd_sends.append(cp)
            n += 1
    for k in range(8):
        x_wait((1 - core) * 8 + k)
    own_copy.wait()

    def split(i, carry):
        rows = pl.ds(pl.multiple_of(i * bl, 8), bl)
        v = xbuf[i].astype(F32)
        xf[rows, :] = v[:bl]
        cf[rows, :] = v[bl:]
        return carry

    lax.fori_loop(0, 16, split, 0)

    common = c_ref[0]
    others = [(common + 1 + j) % EXPERTS for j in range(EXPERTS - 1)]
    rt = 32

    def prep(i, carry):
        rows = pl.ds(pl.multiple_of(i * rt, rt), rt)
        m = meta_ref[rows, :]
        cc, co, oid = m[:, 0:1], m[:, 1:2], m[:, 2:3]
        xv, cv = xf[rows, :], cf[rows, :]
        rc = (cc * cv).astype(BF).astype(F32)
        ro = (co * cv).astype(BF).astype(F32)
        xs[rows, :] = xv.astype(BF)
        rgc[rows, :] = rc.astype(BF)
        rgo[rows, :] = ro.astype(BF)
        for j, e in enumerate(others):
            hit = oid == e.astype(F32)
            xm[j, rows, :] = jnp.where(hit, xv, 0.0).astype(BF)
            rgm[j, rows, :] = jnp.where(hit, ro, 0.0).astype(BF)
        for e in range(EXPERTS):
            hit = (oid == float(e)).astype(F32)
            mo[e, rows, :] = jnp.broadcast_to(hit, (rt, fc)).astype(BF)
        cb[0, rows, :] = jnp.broadcast_to(cc, (rt, 256))
        cb[1, rows, :] = jnp.broadcast_to(co, (rt, 256))
        return carry

    lax.fori_loop(0, tokens // rt, prep, 0)

    for e in range(EXPERTS):
        pltpu.make_async_copy(wg_hbm.at[e], wgu.at[0, e], w_sem.at[0, e]).wait()
        pltpu.make_async_copy(wu_hbm.at[e], wgu.at[1, e], w_sem.at[1, e]).wait()
        pltpu.make_async_copy(wd_hbm.at[e], wd.at[e], w_sem.at[2, e]).wait()

    my = pl.ds(pl.multiple_of(yl * half, half), half)
    his = pl.ds(pl.multiple_of((1 - yl) * half, half), half)
    h1, h2 = pl.ds(0, half), pl.ds(half, half)
    q1, q2 = pl.ds(0, quart), pl.ds(quart, quart)

    def by(r):
        return sec(pb.at[r, :, his], rby.at[r], b_send.at[r], b_recv.at[r], yp)

    ar0 = sec(pa.at[0, :, h1], rar.at[0], a_send.at[0], a_recv.at[0], zp)
    ar1 = sec(pa.at[0, :, h2], rar.at[1], a_send.at[1], a_recv.at[1], zm)
    af0b = sec(pa.at[1, :, h2], raf.at[0, :, h2], a_send.at[2], a_recv.at[2], zp)
    af0a = sec(pa.at[1, :, h1], raf.at[0, :, h1], a_send.at[3], a_recv.at[3], zp)
    af1a = sec(pa.at[2, :, h1], raf.at[1, :, h1], a_send.at[4], a_recv.at[4], zm)
    af1b = sec(pa.at[2, :, h2], raf.at[1, :, h2], a_send.at[5], a_recv.at[5], zm)
    ay = sec(sa, ray, a_send.at[6], a_recv.at[6], yp)

    def chunk(r, carry):
        off = 2 - r + 3 * (r // 2) - 2 * (r // 3)
        zc = (z + off) % NZ
        cols = pl.ds(pl.multiple_of(zc * fc, fc), fc)

        def proj_o(a, c2):
            acc = mm(xm[0], wgu[a, others[0], :, cols])
            acc += mm(xm[1], wgu[a, others[1], :, cols])
            acc += mm(xm[2], wgu[a, others[2], :, cols])
            pbf[r, a] = acc
            pb[r, a] = acc.astype(BF)
            return c2

        lax.fori_loop(0, 2, proj_o, 0)
        acc = mm_nt(rgm[0], wd[others[0], cols, :])
        acc += mm_nt(rgm[1], wd[others[1], cols, :])
        acc += mm_nt(rgm[2], wd[others[2], cols, :])
        pbf[r, 2] = acc
        pb[r, 2] = acc.astype(BF)
        by(r).start()

        def proj_c(a, c2):
            acc = mm(xs[...], wgu[a, common, :, cols])
            paf[r, a] = acc
            pa[r, a] = acc.astype(BF)
            return c2

        lax.fori_loop(0, 2, proj_c, 0)
        acc = mm_nt(rgc[...], wd[common, cols, :])
        paf[r, 2] = acc
        pa[r, 2] = acc.astype(BF)

        @pl.when(r == 0)
        def _():
            ar0.start()
            ar1.start()

        @pl.when(r == 1)
        def _():
            af0b.start()

        @pl.when(r == 2)
        def _():
            af1a.start()

        return carry

    lax.fori_loop(0, NZ, chunk, 0)

    ar0.wait_recv()
    pa[1, :, h1] = (paf[1, :, h1] + rar[0].astype(F32)).astype(BF)
    af0a.start()
    ar1.wait_recv()
    pa[2, :, h2] = (paf[2, :, h2] + rar[1].astype(F32)).astype(BF)
    af1b.start()

    br0 = sec(qb.at[0, :, q1], rbr.at[0], b_send.at[4], b_recv.at[4], zp)
    br1 = sec(qb.at[0, :, q2], rbr.at[1], b_send.at[5], b_recv.at[5], zm)
    bf0b = sec(qb.at[1, :, q2], rbf.at[0, :, q2], b_send.at[6], b_recv.at[6], zp)
    bf0a = sec(qb.at[1, :, q1], rbf.at[0, :, q1], b_send.at[7], b_recv.at[7], zp)
    bf1a = sec(qb.at[2, :, q1], rbf.at[1, :, q1], b_send.at[8], b_recv.at[8], zm)
    bf1b = sec(qb.at[2, :, q2], rbf.at[1, :, q2], b_send.at[9], b_recv.at[9], zm)
    myq1 = pl.ds(pl.multiple_of(yl * half, quart), quart)
    myq2 = pl.ds(pl.multiple_of(yl * half + quart, quart), quart)

    by(0).wait_recv()
    qb[0] = (pbf[0, :, my] + rby[0].astype(F32)).astype(BF)
    br0.start()
    br1.start()
    by(1).wait_recv()
    qb[1, :, q2] = (pbf[1, :, myq2] + rby[1, :, q2].astype(F32)).astype(BF)
    bf0b.start()
    br0.wait_recv()
    qb[1, :, q1] = (
        pbf[1, :, myq1] + rby[1, :, q1].astype(F32) + rbr[0].astype(F32)
    ).astype(BF)
    bf0a.start()
    by(2).wait_recv()
    qb[2, :, q1] = (pbf[2, :, myq1] + rby[2, :, q1].astype(F32)).astype(BF)
    bf1a.start()
    br1.wait_recv()
    qb[2, :, q2] = (
        pbf[2, :, myq2] + rby[2, :, q2].astype(F32) + rbr[1].astype(F32)
    ).astype(BF)
    bf1b.start()
    for cp in (af0b, af0a, af1a, af1b):
        cp.wait_recv()
    sa[...] = (
        paf[3, :, his] + raf[0, :, his].astype(F32) + raf[1, :, his].astype(F32)
    ).astype(BF)
    ay.start()

    def swiglu(total, dst):
        gate, up, dh = total(0), total(1), total(2)
        sg = 1.0 / (1.0 + jnp.exp(-gate))
        act = gate * sg
        dst[z, 0, my, :] = (act * up).astype(BF)
        dst[z, 1, my, :] = (dh * up * sg * (1.0 + gate * (1.0 - sg))).astype(BF)
        dst[z, 2, my, :] = (dh * act).astype(BF)

    by(3).wait_recv()
    for cp in (bf0b, bf0a, bf1a, bf1b):
        cp.wait_recv()
    swiglu(
        lambda a: pbf[3, a, my, :]
        + rby[3, a].astype(F32)
        + rbf[0, a].astype(F32)
        + rbf[1, a].astype(F32),
        ho,
    )

    z1, z3, z2 = (z + 1) % NZ, (z + 3) % NZ, (z + 2) % NZ

    def oz(zc, d, dev):
        return sec(ho.at[zc, :, my], ho.at[zc, :, my], o_send.at[d], o_recv.at[d], dev)

    def oy(zc, i, rows):
        return sec(ho.at[zc, :, rows], ho.at[zc, :, rows], o_send.at[4 + i], o_recv.at[4 + i], yp)

    def orl(zc, rows, d, dev):
        return sec(ho.at[zc, :, rows], ho.at[zc, :, rows], o_send.at[2 + d], o_recv.at[2 + d], dev)

    oz(z, 0, zp).start()
    oz(z, 1, zm).start()
    oy(z, 0, my).start()

    ay.wait_recv()
    swiglu(
        lambda a: paf[3, a, my, :]
        + raf[0, a, my, :].astype(F32)
        + raf[1, a, my, :].astype(F32)
        + ray[a].astype(F32),
        hc,
    )

    def cy(rows):
        return sec(hc.at[z, :, rows], hc.at[z, :, rows], c_send.at[0], c_recv.at[0], yp)

    def cz(zc, h, rows, d, dev):
        i = 1 + 2 * d + h
        return sec(hc.at[zc, :, rows], hc.at[zc, :, rows], c_send.at[i], c_recv.at[i], dev)

    def crl(zc, rows, d, dev):
        return sec(hc.at[zc, :, rows], hc.at[zc, :, rows], c_send.at[5 + d], c_recv.at[5 + d], dev)

    cy(my).start()
    cz(z, yl, my, 0, zp).start()
    cz(z, yl, my, 1, zm).start()

    oz(z3, 0, zp).wait_recv()
    orl(z3, myq1, 0, zp).start()
    oy(z3, 1, my).start()
    oz(z1, 1, zm).wait_recv()
    orl(z1, myq2, 1, zm).start()
    oy(z1, 2, my).start()
    cy(his).wait_recv()
    cz(z, 1 - yl, his, 0, zp).start()
    cz(z, 1 - yl, his, 1, zm).start()

    xf[...] = jnp.zeros_like(xf)
    cf[...] = jnp.zeros_like(cf)

    def dd_copy(par, e, zc):
        rows = pl.ds(pl.multiple_of(zc * fc, fc), fc)
        return pltpu.make_async_copy(dd.at[par, e], dd_hbm.at[e, rows], dd_sem.at[par, e])

    def second(r, carry):
        off = 3 * r - 5 * (r // 2) - 2 * (r // 3)
        zc = (z + off) % NZ
        cols = pl.ds(pl.multiple_of(zc * fc, fc), fc)
        par = r % 2

        @pl.when(r == 0)
        def _():
            oy(z, 0, his).wait_recv()

        @pl.when(r == 1)
        def _():
            orl(z2, myq1, 0, zp).wait_recv()
            orl(z2, myq2, 1, zm).wait_recv()
            oy(z2, 3, my).start()
            cz(z3, 0, h1, 0, zp).wait_recv()
            crl(z3, h1, 0, zp).start()
            cz(z1, 1, h2, 1, zm).wait_recv()
            crl(z1, h2, 1, zm).start()
            cz(z3, 1, h2, 0, zp).wait_recv()
            oy(z3, 1, his).wait_recv()

        @pl.when(r == 2)
        def _():
            cz(z1, 0, h1, 1, zm).wait_recv()
            oy(z1, 2, his).wait_recv()

        @pl.when(r == 3)
        def _():
            crl(z2, h1, 0, zp).wait_recv()
            crl(z2, h2, 1, zm).wait_recv()
            oy(z2, 3, his).wait_recv()

        def expert(e, c2):
            is_c = (common == e).astype(F32)
            mc = is_c.astype(BF)
            hit = mo[e]
            hs = hc[zc, 0] * mc + ho[zc, 0] * hit
            dgs = hc[zc, 1] * mc + ho[zc, 1] * hit
            dus = hc[zc, 2] * mc + ho[zc, 2] * hit
            comb = cb[0] * is_c + cb[1] * (1.0 - is_c)

            @pl.when(r >= 2)
            def _():
                dd_copy(par, e, zc).wait()

            for i in range(nt):
                ns = pl.ds(i * 256, 256)
                xf[:, ns] += comb * mm(hs, wd[e, cols, ns])
                cf[:, ns] += mm_nt(dgs, wgu[0, e, ns, cols]) + mm_nt(dus, wgu[1, e, ns, cols])
                rgs = rgc[:, ns] * mc + rgo[:, ns] * (1.0 - is_c).astype(BF)
                dd[par, e, :, ns] = mm_tn(hs, rgs).astype(BF)
            dd_copy(par, e, zc).start()
            return c2

        lax.fori_loop(0, EXPERTS, expert, 0)
        return carry

    lax.fori_loop(0, NZ, second, 0)

    mine = pl.ds(pl.multiple_of(core * half, half), half)
    theirs = pl.ds(pl.multiple_of((1 - core) * half, half), half)
    fs[0] = xf[theirs, :].astype(BF)
    fs[1] = cf[theirs, :].astype(BF)
    pair = ten(fs, fr, f_send.at[0], f_recv.at[8], sib)
    pair.start()
    pair.wait_recv()
    xf[mine, :] += fr[0].astype(F32)
    cf[mine, :] += fr[1].astype(F32)

    def rows_of(k):
        return pl.ds(pl.multiple_of(core * half + k * bl, 8), bl)

    def both(k):
        return jnp.concatenate([xf[rows_of(k), :], cf[rows_of(k), :]], 0)

    def out_send(k):
        return ten(gs.at[k], gr.at[kt], f_send.at[k], f_recv.at[kt], k * 2 + core)

    def send(i, carry):
        k = (kt + i) % 8
        gs[k] = both(k).astype(BF)
        out_send(k).start()
        return carry

    pair.wait_send()
    lax.fori_loop(1, 8, send, 0)
    total = both(kt)
    for i in range(1, 8):
        k = (kt + i) % 8
        ten(gs.at[k], gr.at[k], f_send.at[k], f_recv.at[k], k * 2 + core).wait_recv()
        total += gr[k].astype(F32)
    lo_ref[...] = total[:bl].astype(BF)
    dt_ref[...] = total[bl:].astype(BF)

    for i in range(1, 8):
        out_send((kt + i) % 8).wait_send()
    for e in range(EXPERTS):
        dd_copy(0, e, z1).wait()
        dd_copy(1, e, z2).wait()
    for cp in own_sends + fwd_sends:
        cp.wait_send()
    for r in range(NZ):
        by(r).wait_send()
    for cp in (ar0, ar1, af0a, af0b, af1a, af1b, ay, br0, br1, bf0a, bf0b, bf1a, bf1b):
        cp.wait_send()
    oz(z, 0, zp).wait_send()
    oz(z, 1, zm).wait_send()
    orl(z3, myq1, 0, zp).wait_send()
    orl(z1, myq2, 1, zm).wait_send()
    for i, zc in enumerate((z, z3, z1, z2)):
        oy(zc, i, my).wait_send()
    cy(my).wait_send()
    for h, rows in ((yl, my), (1 - yl, his)):
        cz(z, h, rows, 0, zp).wait_send()
        cz(z, h, rows, 1, zm).wait_send()
    crl(z3, h1, 0, zp).wait_send()
    crl(z1, h2, 1, zm).wait_send()


def on_device(tokens, combine, expert_ids, expert_counts, w_gate, w_up, w_down, cotangent):
    total = combine.shape[0]
    bl, dloc = tokens.shape
    floc = w_gate.shape[2]
    fc = floc // NZ
    half, quart = total // 2, total // 4
    common = jnp.argmax(expert_counts == total).astype(jnp.int32)
    is_common = expert_ids == common
    comb_c = jnp.sum(jnp.where(is_common, combine, 0.0), 1)
    comb_o = jnp.sum(jnp.where(is_common, 0.0, combine), 1)
    other = jnp.sum(jnp.where(is_common, 0, expert_ids), 1).astype(F32)
    meta = jnp.stack([comb_c, comb_o, other, other], 1)
    meta = meta.reshape(8, 2, bl, 4).transpose(1, 0, 2, 3).reshape(total, 4)
    xt = jnp.concatenate([tokens, cotangent], 0)
    any_spec = pl.BlockSpec(memory_space=pl.ANY)
    vmem = pl.BlockSpec(memory_space=pltpu.VMEM)
    V = pltpu.VMEM
    dma = pltpu.SemaphoreType.DMA
    return pl.pallas_call(
        layer_kernel,
        out_shape=(
            jax.ShapeDtypeStruct((bl, dloc), BF),
            jax.ShapeDtypeStruct((bl, dloc), BF),
            jax.ShapeDtypeStruct((EXPERTS, floc, dloc), BF),
        ),
        in_specs=[pl.BlockSpec(memory_space=pltpu.SMEM), vmem, vmem, any_spec, any_spec, any_spec],
        out_specs=(vmem, vmem, any_spec),
        scratch_shapes=[
            V((2, EXPERTS, dloc, floc), BF),
            V((EXPERTS, floc, dloc), BF),
            V((16, 2 * bl, dloc), BF),
            V((total, dloc), F32),
            V((total, dloc), F32),
            V((total, dloc), BF),
            V((EXPERTS - 1, total, dloc), BF),
            V((total, dloc), BF),
            V((total, dloc), BF),
            V((EXPERTS - 1, total, dloc), BF),
            V((EXPERTS, total, fc), BF),
            V((2, total, 256), F32),
            V((NZ, 3, total, fc), BF),
            V((NZ, 3, total, fc), F32),
            V((NZ, 3, total, fc), BF),
            V((NZ, 3, total, fc), F32),
            V((2, 3, half, fc), BF),
            V((2, 3, total, fc), BF),
            V((3, half, fc), BF),
            V((3, half, fc), BF),
            V((NZ, 3, half, fc), BF),
            V((3, 3, half, fc), BF),
            V((2, 3, quart, fc), BF),
            V((2, 3, half, fc), BF),
            V((NZ, 3, total, fc), BF),
            V((NZ, 3, total, fc), BF),
            V((2, EXPERTS, fc, dloc), BF),
            V((2, half, dloc), BF),
            V((2, half, dloc), BF),
            V((8, 2 * bl, dloc), BF),
            V((8, 2 * bl, dloc), BF),
            dma((3, EXPERTS)),
            dma,
            dma((15,)),
            dma((16,)),
            dma((7,)),
            dma((7,)),
            dma((10,)),
            dma((10,)),
            dma((7,)),
            dma((7,)),
            dma((8,)),
            dma((8,)),
            dma((2, EXPERTS)),
            dma((8,)),
            dma((9,)),
        ],
        compiler_params=pltpu.CompilerParams(
            collective_id=0, has_side_effects=True, vmem_limit_bytes=67043328
        ),
    )(common.reshape(1), meta, xt, w_gate, w_up, w_down)


def solution(mesh):
    in_specs = (
        P("tensor", "section"),
        P(),
        P(),
        P(),
        P(None, "section", "tensor"),
        P(None, "section", "tensor"),
        P(None, "tensor", "section"),
        P("tensor", "section"),
    )
    out_specs = (P("tensor", "section"), P("tensor", "section"), P(None, "tensor", "section"))
    return jax.shard_map(
        on_device, mesh=mesh, in_specs=in_specs, out_specs=out_specs, check_vma=False
    )
```

```python
import jax
import jax.numpy as jnp
from jax import lax
from jax.experimental import pallas as pl
from jax.experimental.pallas import tpu as pltpu
from jax.sharding import PartitionSpec as P

EXPERTS = 4
NZ = 4
VLIM = 60000000
BF = jnp.bfloat16
F32 = jnp.float32
MESH = pl.DeviceIdType.MESH


def mm(a, b):
    return jnp.dot(a, b, preferred_element_type=F32)


def mm_nt(a, b):
    return lax.dot_general(a, b, (((1,), (1,)), ((), ())), preferred_element_type=F32)


def mm_tn(a, b):
    return lax.dot_general(a, b, (((0,), (0,)), ((), ())), preferred_element_type=F32)


def layer_kernel(
    counts_ref, comb_ref, ids_ref, tok_ref, cot_ref, wg_hbm, wu_hbm, wd_hbm,
    lo_ref, dt_ref, dd_ref,
    wgu, wd, tbuf, cbuf, meta, xf, cf, xs, xm, rgc, rgo, rgm, mo, cb,
    pa, paf, pb, pbf, rar, raf, sa, ray, rby, qb, rbr, rbf, hc, ho, fs, fr, gs, gr,
    w_sem, loc_sem, x_send, x_recv, a_send, a_recv, b_send, b_recv,
    c_send, c_recv, o_send, o_recv, p_send, p_recv, f_send, f_recv,
):
    tokens, dloc = xf.shape
    fc = pa.shape[-1]
    half = tokens // 2
    quart = half // 2
    bl = tokens // 16
    nt = dloc // 256

    s = lax.axis_index("section")
    t = lax.axis_index("tensor")
    z, yl = s // 2, s % 2
    zp = ((z + 1) % NZ) * 2 + yl
    zm = ((z + 3) % NZ) * 2 + yl
    yp = z * 2 + 1 - yl
    zdev = (zp, zm)
    core, kt, x = t % 2, t // 2, t // 4
    yh = kt % 2

    def tx(d):
        return ((x + d) % 4) * 4 + yh * 2 + core

    ty = x * 4 + (1 - yh) * 2 + core
    sib = t + 1 - 2 * core

    def sec(src, dst, ssem, rsem, dev):
        return pltpu.make_async_remote_copy(src, dst, ssem, rsem, {"section": dev}, MESH)

    def ten(src, dst, ssem, rsem, dev):
        return pltpu.make_async_remote_copy(src, dst, ssem, rsem, {"tensor": dev}, MESH)

    def w_copy(a, e):
        if a == 2:
            return pltpu.make_async_copy(wd_hbm.at[e], wd.at[e], w_sem.at[2, e])
        return pltpu.make_async_copy((wg_hbm, wu_hbm)[a].at[e], wgu.at[a, e], w_sem.at[a, e])

    for a in range(3):
        for e in range(EXPERTS):
            w_copy(a, e).start()

    barrier = pltpu.get_barrier_semaphore()
    for dev in (zp, zm, yp):
        pl.semaphore_signal(barrier, inc=1, device_id={"section": dev}, device_id_type=MESH)
    for k in range(1, 8):
        pl.semaphore_signal(
            barrier, inc=1, device_id={"tensor": ((kt + k) % 8) * 2 + core}, device_id_type=MESH
        )
    pl.semaphore_signal(barrier, inc=1, device_id={"tensor": sib}, device_id_type=MESH)
    pl.semaphore_wait(barrier, 11)

    q = core * 8 + kt
    qy = core * 8 + x * 2 + 1 - yh
    targets = (ty, tx(1), tx(3), tx(2), sib)
    bufs = (tbuf, cbuf)
    srcs = (tok_ref, cot_ref)
    slots = [
        core * 8 + ((x + d) % 4) * 2 + yh + flip - 2 * yh * flip for flip in (0, 1) for d in (1, 3, 2)
    ]

    def own_copy(g):
        return pltpu.make_async_copy(srcs[g], bufs[g].at[q], loc_sem.at[g])

    def own_send(g, i):
        return ten(srcs[g], bufs[g].at[q], x_send.at[g, i], x_recv.at[g, q], targets[i])

    def pass_on(g, i, slot, dev):
        return ten(bufs[g].at[slot], bufs[g].at[slot], x_send.at[g, i], x_recv.at[g, slot], dev)

    def gather_start(g):
        own_copy(g).start()
        for i in range(5):
            own_send(g, i).start()

    def gather_mid(g):
        pass_on(g, 0, qy, sib).wait_recv()
        for i in range(4):
            pass_on(g, 5 + i, qy, targets[1 + i]).start()

    def gather_pair(g):
        for i in range(6):
            pass_on(g, 0, slots[i], sib).wait_recv()
            pass_on(g, 9 + i, slots[i], sib).start()

    def gather_end(g):
        for k in range(8):
            pass_on(g, 0, (1 - core) * 8 + k, sib).wait_recv()
        own_copy(g).wait()

    gather_start(0)

    common = jnp.int32(EXPERTS - 1)
    for e in range(EXPERTS - 2, -1, -1):
        common = jnp.where(counts_ref[e] == tokens, e, common)
    others = [(common + 1 + j) % EXPERTS for j in range(EXPERTS - 1)]
    ids, cmb = ids_ref[...], comb_ref[...]
    is_c = ids == common
    cc_row = jnp.sum(jnp.where(is_c, cmb, 0.0), 0, keepdims=True)
    co_row = jnp.sum(jnp.where(is_c, 0.0, cmb), 0, keepdims=True)
    id_row = jnp.sum(jnp.where(is_c, 0.0, ids.astype(F32)), 0, keepdims=True)
    which = lax.broadcasted_iota(jnp.int32, (128, tokens), 0)
    grid = jnp.where(which == 0, cc_row, jnp.where(which == 1, co_row, id_row))
    columns = grid.T
    for i in range(16):
        at = (i % 2) * 8 + i // 2
        meta[at * bl : (at + 1) * bl, :] = columns[i * bl : (i + 1) * bl, :]

    gather_mid(0)
    gather_pair(0)
    gather_end(0)
    gather_start(1)

    rt = 32

    def spread(buf, dst):
        def split(i, carry):
            dst[pl.ds(pl.multiple_of(i * bl, 8), bl), :] = buf[i].astype(F32)
            return carry

        lax.fori_loop(0, 16, split, 0)

    def prep_x(i, carry):
        rows = pl.ds(pl.multiple_of(i * rt, rt), rt)
        oid = meta[rows, 2:3]
        xv = xf[rows, :]
        xs[rows, :] = xv.astype(BF)
        for j, e in enumerate(others):
            xm[j, rows, :] = jnp.where(oid == e.astype(F32), xv, 0.0).astype(BF)
        return carry

    def prep_c(i, carry):
        rows = pl.ds(pl.multiple_of(i * rt, rt), rt)
        m = meta[rows, :]
        cc, co, oid = m[:, 0:1], m[:, 1:2], m[:, 2:3]
        cv = cf[rows, :]
        ro = (co * cv).astype(BF).astype(F32)
        rgc[rows, :] = (cc * cv).astype(BF)
        rgo[rows, :] = ro.astype(BF)
        for j, e in enumerate(others):
            rgm[j, rows, :] = jnp.where(oid == e.astype(F32), ro, 0.0).astype(BF)
        for e in range(EXPERTS):
            hit = (oid == float(e)).astype(F32)
            mo[e, rows, :] = jnp.broadcast_to(hit, (rt, fc)).astype(BF)
        cb[0, rows, :] = jnp.broadcast_to(cc, (rt, 256))
        cb[1, rows, :] = jnp.broadcast_to(co, (rt, 256))
        return carry

    spread(tbuf, xf)
    lax.fori_loop(0, tokens // rt, prep_x, 0)
    for a in range(2):
        for e in range(EXPERTS):
            w_copy(a, e).wait()

    my = pl.ds(pl.multiple_of(yl * half, half), half)
    his = pl.ds(pl.multiple_of((1 - yl) * half, half), half)
    hh = (pl.ds(0, half), pl.ds(half, half))
    qq = (pl.ds(0, quart), pl.ds(quart, quart))
    mq = (
        pl.ds(pl.multiple_of(yl * half, quart), quart),
        pl.ds(pl.multiple_of(yl * half + quart, quart), quart),
    )
    gg = (pl.ds(0, 2), pl.ds(2, 1))

    def by(g, r):
        return sec(pb.at[r, gg[g], his], rby.at[r, gg[g]], b_send.at[g, r], b_recv.at[g, r], yp)

    def ar(g, d):
        return sec(
            pa.at[0, gg[g], hh[d]], rar.at[d, gg[g]], a_send.at[g, d], a_recv.at[g, d], zdev[d]
        )

    def af(g, d, h):
        i = 2 + 2 * d + h
        return sec(
            pa.at[1 + d, gg[g], hh[h]], raf.at[d, gg[g], hh[h]], a_send.at[g, i], a_recv.at[g, i],
            zdev[d],
        )

    def ay(g):
        return sec(sa.at[gg[g]], ray.at[gg[g]], a_send.at[g, 6], a_recv.at[g, 6], yp)

    def br(g, d):
        i = 4 + d
        return sec(
            qb.at[0, gg[g], qq[d]], rbr.at[d, gg[g]], b_send.at[g, i], b_recv.at[g, i], zdev[d]
        )

    def bf(g, d, h):
        i = 6 + 2 * d + h
        return sec(
            qb.at[1 + d, gg[g], qq[h]], rbf.at[d, gg[g], qq[h]], b_send.at[g, i], b_recv.at[g, i],
            zdev[d],
        )

    def chunk_of(r):
        zc = (z + 2 - r + 3 * (r // 2) - 2 * (r // 3)) % NZ
        return pl.ds(pl.multiple_of(zc * fc, fc), fc)

    def leave(g, r):
        @pl.when(r == 0)
        def _():
            ar(g, 0).start()
            ar(g, 1).start()

        @pl.when(r == 1)
        def _():
            af(g, 0, 1).start()

        @pl.when(r == 2)
        def _():
            af(g, 1, 0).start()

    def first_gu(r, carry):
        cols = chunk_of(r)

        @pl.when(r == 2)
        def _():
            gather_mid(1)

        def proj_o(a, c2):
            acc = mm(xm[0], wgu[a, others[0], :, cols])
            acc += mm(xm[1], wgu[a, others[1], :, cols])
            acc += mm(xm[2], wgu[a, others[2], :, cols])
            pbf[r, a] = acc
            pb[r, a] = acc.astype(BF)
            return c2

        lax.fori_loop(0, 2, proj_o, 0)
        by(0, r).start()

        def proj_c(a, c2):
            acc = mm(xs[...], wgu[a, common, :, cols])
            paf[r, a] = acc
            pa[r, a] = acc.astype(BF)
            return c2

        lax.fori_loop(0, 2, proj_c, 0)
        leave(0, r)
        return carry

    def first_dh(r, carry):
        cols = chunk_of(r)
        acc = mm_nt(rgm[0], wd[others[0], cols, :])
        acc += mm_nt(rgm[1], wd[others[1], cols, :])
        acc += mm_nt(rgm[2], wd[others[2], cols, :])
        pbf[r, 2] = acc
        pb[r, 2] = acc.astype(BF)
        by(1, r).start()
        acc = mm_nt(rgc[...], wd[common, cols, :])
        paf[r, 2] = acc
        pa[r, 2] = acc.astype(BF)
        leave(1, r)
        return carry

    def a_relay(g):
        for d in (0, 1):
            ar(g, d).wait_recv()
            pa[1 + d, gg[g], hh[d]] = (
                paf[1 + d, gg[g], hh[d]] + rar[d, gg[g]].astype(F32)
            ).astype(BF)
            af(g, d, d).start()

    def a_final(g):
        for d in (0, 1):
            for h in (0, 1):
                af(g, d, h).wait_recv()
        sa[gg[g]] = (
            paf[3, gg[g], his]
            + raf[0, gg[g], his].astype(F32)
            + raf[1, gg[g], his].astype(F32)
        ).astype(BF)
        ay(g).start()

    def b_step(g, r):
        by(g, r).wait_recv()
        if r == 0:
            qb[0, gg[g]] = (pbf[0, gg[g], my] + rby[0, gg[g]].astype(F32)).astype(BF)
            br(g, 0).start()
            br(g, 1).start()
        elif r < 3:
            d = r - 1
            h = 1 - d
            qb[r, gg[g], qq[h]] = (
                pbf[r, gg[g], mq[h]] + rby[r, gg[g], qq[h]].astype(F32)
            ).astype(BF)
            bf(g, d, h).start()
            br(g, d).wait_recv()
            qb[r, gg[g], qq[d]] = (
                pbf[r, gg[g], mq[d]]
                + rby[r, gg[g], qq[d]].astype(F32)
                + rbr[d, gg[g]].astype(F32)
            ).astype(BF)
            bf(g, d, d).start()

    lax.fori_loop(0, NZ, first_gu, 0)
    gather_pair(1)
    a_relay(0)
    b_step(0, 0)
    gather_end(1)
    spread(cbuf, cf)
    lax.fori_loop(0, tokens // rt, prep_c, 0)
    for e in range(EXPERTS):
        w_copy(2, e).wait()
    lax.fori_loop(0, NZ, first_dh, 0)
    b_step(0, 1)
    a_relay(1)
    b_step(0, 2)
    a_final(0)
    b_step(0, 3)
    b_step(1, 0)
    b_step(1, 1)
    b_step(1, 2)
    a_final(1)
    b_step(1, 3)

    def swiglu(total, dst):
        gate, up, dh = total(0), total(1), total(2)
        sg = 1.0 / (1.0 + jnp.exp(-gate))
        act = gate * sg
        dst[z, 0, my, :] = (act * up).astype(BF)
        dst[z, 1, my, :] = (dh * up * sg * (1.0 + gate * (1.0 - sg))).astype(BF)
        dst[z, 2, my, :] = (dh * act).astype(BF)

    for g in (0, 1):
        for d in (0, 1):
            for h in (0, 1):
                bf(g, d, h).wait_recv()
    swiglu(
        lambda a: pbf[3, a, my, :]
        + rby[3, a].astype(F32)
        + rbf[0, a].astype(F32)
        + rbf[1, a].astype(F32),
        ho,
    )

    z1, z3, z2 = (z + 1) % NZ, (z + 3) % NZ, (z + 2) % NZ

    def oz(zc, d):
        return sec(ho.at[zc, :, my], ho.at[zc, :, my], o_send.at[d], o_recv.at[d], zdev[d])

    def oy(zc, i, rows):
        return sec(ho.at[zc, :, rows], ho.at[zc, :, rows], o_send.at[4 + i], o_recv.at[4 + i], yp)

    def orl(zc, d):
        part = ho.at[zc, :, mq[d]]
        return sec(part, part, o_send.at[2 + d], o_recv.at[2 + d], zdev[d])

    oz(z, 0).start()
    oz(z, 1).start()
    oy(z, 0, my).start()

    ay(0).wait_recv()
    ay(1).wait_recv()
    swiglu(
        lambda a: paf[3, a, my, :]
        + raf[0, a, my, :].astype(F32)
        + raf[1, a, my, :].astype(F32)
        + ray[a].astype(F32),
        hc,
    )

    def cy(rows):
        return sec(hc.at[z, :, rows], hc.at[z, :, rows], c_send.at[0], c_recv.at[0], yp)

    def cz(zc, h, rows, d):
        i = 1 + 2 * d + h
        return sec(hc.at[zc, :, rows], hc.at[zc, :, rows], c_send.at[i], c_recv.at[i], zdev[d])

    def crl(zc, d):
        part = hc.at[zc, :, hh[d]]
        return sec(part, part, c_send.at[5 + d], c_recv.at[5 + d], zdev[d])

    cy(my).start()
    cz(z, yl, my, 0).start()
    cz(z, yl, my, 1).start()

    oz(z3, 0).wait_recv()
    orl(z3, 0).start()
    oy(z3, 1, my).start()
    oz(z1, 1).wait_recv()
    orl(z1, 1).start()
    oy(z1, 2, my).start()
    cy(his).wait_recv()
    cz(z, 1 - yl, his, 0).start()
    cz(z, 1 - yl, his, 1).start()

    xf[...] = jnp.zeros_like(xf)
    cf[...] = jnp.zeros_like(cf)
    for g in (0, 1):
        for r in range(NZ):
            by(g, r).wait_send()

    mine = pl.ds(pl.multiple_of(core * half, half), half)
    theirs = pl.ds(pl.multiple_of((1 - core) * half, half), half)

    def tile(i):
        return pl.ds(pl.multiple_of(i * 256, 256), 256)

    def pair(i):
        return ten(fs.at[i], fr.at[i], p_send.at[i], p_recv.at[i], sib)

    def out_send(i, k):
        return ten(gs.at[i, k], gr.at[i, kt], f_send.at[i, k], f_recv.at[i, kt], k * 2 + core)

    def both(i, k):
        rows = pl.ds(pl.multiple_of(core * half + k * bl, 8), bl)
        return jnp.concatenate([xf[rows, tile(i)], cf[rows, tile(i)]], 0)

    def flush(i):
        pair(i).wait_recv()
        xf[mine, tile(i)] += fr[i, 0].astype(F32)
        cf[mine, tile(i)] += fr[i, 1].astype(F32)

        def send(n, carry):
            k = (kt + n) % 8
            gs[i, k] = both(i, k).astype(BF)
            out_send(i, k).start()
            return carry

        lax.fori_loop(1, 8, send, 0)

    def second(r, carry):
        zc = (z + 3 * r - 5 * (r // 2) - 2 * (r // 3)) % NZ
        cols = pl.ds(pl.multiple_of(zc * fc, fc), fc)

        @pl.when(r == 1)
        def _():
            for d in (0, 1):
                orl(z2, d).wait_recv()
            oy(z2, 3, my).start()
            cz(z3, 0, hh[0], 0).wait_recv()
            crl(z3, 0).start()
            cz(z1, 1, hh[1], 1).wait_recv()
            crl(z1, 1).start()
            cz(z3, 1, hh[1], 0).wait_recv()

        @pl.when(r == 2)
        def _():
            cz(z1, 0, hh[0], 1).wait_recv()

        @pl.when(r == 3)
        def _():
            crl(z2, 0).wait_recv()
            crl(z2, 1).wait_recv()

        def common_tile(i, c2):
            ns = tile(i)
            xf[:, ns] += cb[0] * mm(hc[zc, 0], wd[common, cols, ns])
            cf[:, ns] += mm_nt(hc[zc, 1], wgu[0, common, ns, cols]) + mm_nt(
                hc[zc, 2], wgu[1, common, ns, cols]
            )
            return c2

        lax.fori_loop(0, nt, common_tile, 0)

        @pl.when(r == 0)
        def _():
            oy(z, 0, his).wait_recv()

        @pl.when(r == 1)
        def _():
            oy(z3, 1, his).wait_recv()

        @pl.when(r == 2)
        def _():
            oy(z1, 2, his).wait_recv()

        @pl.when(r == 3)
        def _():
            oy(z2, 3, his).wait_recv()

        for j, e in enumerate(others):
            hit = mo[e]
            for a in range(3):
                pb[j, a] = ho[zc, a] * hit

        def other_tile(i, c2):
            ns = tile(i)
            acc = mm(pb[0, 0], wd[others[0], cols, ns])
            acc += mm(pb[1, 0], wd[others[1], cols, ns])
            acc += mm(pb[2, 0], wd[others[2], cols, ns])
            xf[:, ns] += cb[1] * acc
            acc = mm_nt(pb[0, 1], wgu[0, others[0], ns, cols])
            acc += mm_nt(pb[0, 2], wgu[1, others[0], ns, cols])
            for j in (1, 2):
                acc += mm_nt(pb[j, 1], wgu[0, others[j], ns, cols])
                acc += mm_nt(pb[j, 2], wgu[1, others[j], ns, cols])
            cf[:, ns] += acc

            @pl.when(r == 3)
            def _():
                fs[i, 0] = xf[theirs, ns].astype(BF)
                fs[i, 1] = cf[theirs, ns].astype(BF)
                pair(i).start()

                @pl.when(i > 0)
                def _():
                    flush(i - 1)

            return c2

        lax.fori_loop(0, nt, other_tile, 0)
        return carry

    lax.fori_loop(0, NZ, second, 0)
    flush(nt - 1)

    def weight_grad(e, carry):
        here = (common == e).astype(F32)
        mc = here.astype(BF)
        hit = mo[e]
        xs[...] = rgc[...] * mc + rgo[...] * (1.0 - here).astype(BF)

        def block(zc, c2):
            hs = hc[zc, 0] * mc + ho[zc, 0] * hit
            rows = pl.ds(pl.multiple_of(zc * fc, fc), fc)
            for i in range(nt):
                ns = pl.ds(i * 256, 256)
                dd_ref[e, rows, ns] = mm_tn(hs, xs[:, ns]).astype(BF)
            return c2

        lax.fori_loop(0, NZ, block, 0)
        return carry

    lax.fori_loop(0, EXPERTS, weight_grad, 0)

    for i in range(nt):
        total = both(i, kt)
        for n in range(1, 8):
            k = (kt + n) % 8
            dev = k * 2 + core
            ten(gs.at[i, k], gr.at[i, k], f_send.at[i, k], f_recv.at[i, k], dev).wait_recv()
            total += gr[i, k].astype(F32)
        lo_ref[:, i * 256 : (i + 1) * 256] = total[:bl].astype(BF)
        dt_ref[:, i * 256 : (i + 1) * 256] = total[bl:].astype(BF)

    for i in range(nt):
        pair(i).wait_send()
        for n in range(1, 8):
            out_send(i, (kt + n) % 8).wait_send()
    for g in (0, 1):
        for i in range(5):
            own_send(g, i).wait_send()
        for i in range(4):
            pass_on(g, 5 + i, qy, targets[1 + i]).wait_send()
        for i in range(6):
            pass_on(g, 9 + i, slots[i], sib).wait_send()
        for d in (0, 1):
            ar(g, d).wait_send()
            br(g, d).wait_send()
            for h in (0, 1):
                af(g, d, h).wait_send()
                bf(g, d, h).wait_send()
        ay(g).wait_send()
    for d, zc in ((0, z3), (1, z1)):
        oz(z, d).wait_send()
        orl(zc, d).wait_send()
        crl(zc, d).wait_send()
        cz(z, yl, my, d).wait_send()
        cz(z, 1 - yl, his, d).wait_send()
    for i, zc in enumerate((z, z3, z1, z2)):
        oy(zc, i, my).wait_send()
    cy(my).wait_send()


def on_device(tokens, combine, expert_ids, expert_counts, w_gate, w_up, w_down, cotangent):
    total = combine.shape[0]
    bl, dloc = tokens.shape
    floc = w_gate.shape[2]
    fc = floc // NZ
    half, quart = total // 2, total // 4
    nt = dloc // 256
    any_spec = pl.BlockSpec(memory_space=pl.ANY)
    vmem = pl.BlockSpec(memory_space=pltpu.VMEM)
    V = pltpu.VMEM
    dma = pltpu.SemaphoreType.DMA
    return pl.pallas_call(
        layer_kernel,
        out_shape=(V((bl, dloc), BF), V((bl, dloc), BF), V((EXPERTS, floc, dloc), BF)),
        in_specs=[pl.BlockSpec(memory_space=pltpu.SMEM)] + [vmem] * 4 + [any_spec] * 3,
        out_specs=(vmem, vmem, vmem),
        scratch_shapes=[
            V((2, EXPERTS, dloc, floc), BF),
            V((EXPERTS, floc, dloc), BF),
            V((16, bl, dloc), BF),
            V((16, bl, dloc), BF),
            V((total, 128), F32),
            V((total, dloc), F32),
            V((total, dloc), F32),
            V((total, dloc), BF),
            V((EXPERTS - 1, total, dloc), BF),
            V((total, dloc), BF),
            V((total, dloc), BF),
            V((EXPERTS - 1, total, dloc), BF),
            V((EXPERTS, total, fc), BF),
            V((2, total, 256), F32),
            V((NZ, 3, total, fc), BF),
            V((NZ, 3, total, fc), F32),
            V((NZ, 3, total, fc), BF),
            V((NZ, 3, total, fc), F32),
            V((2, 3, half, fc), BF),
            V((2, 3, total, fc), BF),
            V((3, half, fc), BF),
            V((3, half, fc), BF),
            V((NZ, 3, half, fc), BF),
            V((3, 3, half, fc), BF),
            V((2, 3, quart, fc), BF),
            V((2, 3, half, fc), BF),
            V((NZ, 3, total, fc), BF),
            V((NZ, 3, total, fc), BF),
            V((nt, 2, half, 256), BF),
            V((nt, 2, half, 256), BF),
            V((nt, 8, 2 * bl, 256), BF),
            V((nt, 8, 2 * bl, 256), BF),
            dma((3, EXPERTS)),
            dma((2,)),
            dma((2, 15)),
            dma((2, 16)),
            dma((2, 7)),
            dma((2, 7)),
            dma((2, 10)),
            dma((2, 10)),
            dma((7,)),
            dma((7,)),
            dma((8,)),
            dma((8,)),
            dma((nt,)),
            dma((nt,)),
            dma((nt, 8)),
            dma((nt, 8)),
        ],
        compiler_params=pltpu.CompilerParams(
            collective_id=0, has_side_effects=True, vmem_limit_bytes=VLIM
        ),
    )(expert_counts, combine.T, expert_ids.T, tokens, cotangent, w_gate, w_up, w_down)


def solution(mesh):
    in_specs = (
        P("tensor", "section"),
        P(),
        P(),
        P(),
        P(None, "section", "tensor"),
        P(None, "section", "tensor"),
        P(None, "tensor", "section"),
        P("tensor", "section"),
    )
    out_specs = (P("tensor", "section"), P("tensor", "section"), P(None, "tensor", "section"))
    return jax.shard_map(
        on_device, mesh=mesh, in_specs=in_specs, out_specs=out_specs, check_vma=False
    )
```

```python
import jax
import jax.numpy as jnp
from jax import lax
from jax.experimental import pallas as pl
from jax.experimental.pallas import tpu as pltpu
from jax.sharding import PartitionSpec as P

EXPERTS = 4
NZ = 4
VLIM = 60000000
HOPS = ((2, 1), (1, 1), (3, 1), (0, 1), (2, 0), (1, 0), (3, 0))
ORDER = (5, 6, 4, 3, 1, 2, 0)
BF = jnp.bfloat16
F32 = jnp.float32
MESH = pl.DeviceIdType.MESH


def mm(a, b):
    return jnp.dot(a, b, preferred_element_type=F32)


def mm_nt(a, b):
    return lax.dot_general(a, b, (((1,), (1,)), ((), ())), preferred_element_type=F32)


def mm_tn(a, b):
    return lax.dot_general(a, b, (((0,), (0,)), ((), ())), preferred_element_type=F32)


def layer_kernel(
    counts_ref, comb_ref, ids_ref, tok_ref, cot_ref, wg_hbm, wu_hbm, wd_hbm,
    lo_ref, dt_ref, dd_ref,
    wgu, wd, tbuf, cbuf, meta, xf, cf, xs, xm, rgc, rgo, rgm, mo, cb,
    pa, paf, pb, pbf, rar, raf, sa, ray, rby, qb, rbr, rbf, hc, ho, fs, fr, gs, gr,
    w_sem, loc_sem, x_send, x_recv, a_send, a_recv, b_send, b_recv,
    c_send, c_recv, o_send, o_recv, p_send, p_recv, f_send, f_recv,
):
    tokens, dloc = xf.shape
    fc = pa.shape[-1]
    half = tokens // 2
    quart = half // 2
    bl = tokens // 16
    nt = dloc // 256

    s = lax.axis_index("section")
    t = lax.axis_index("tensor")
    z, yl = s // 2, s % 2
    zp = ((z + 1) % NZ) * 2 + yl
    zm = ((z + 3) % NZ) * 2 + yl
    yp = z * 2 + 1 - yl
    zdev = (zp, zm)
    core, kt, x = t % 2, t // 2, t // 4
    yh = kt % 2

    def tx(d):
        return ((x + d) % 4) * 4 + yh * 2 + core

    ty = x * 4 + (1 - yh) * 2 + core
    sib = t + 1 - 2 * core

    def sec(src, dst, ssem, rsem, dev):
        return pltpu.make_async_remote_copy(src, dst, ssem, rsem, {"section": dev}, MESH)

    def ten(src, dst, ssem, rsem, dev):
        return pltpu.make_async_remote_copy(src, dst, ssem, rsem, {"tensor": dev}, MESH)

    def w_copy(a, e):
        if a == 2:
            return pltpu.make_async_copy(wd_hbm.at[e], wd.at[e], w_sem.at[2, e])
        return pltpu.make_async_copy((wg_hbm, wu_hbm)[a].at[e], wgu.at[a, e], w_sem.at[a, e])

    for a in range(3):
        for e in range(EXPERTS):
            w_copy(a, e).start()

    barrier = pltpu.get_barrier_semaphore()
    for dev in (zp, zm, yp):
        pl.semaphore_signal(barrier, inc=1, device_id={"section": dev}, device_id_type=MESH)
    for k in range(1, 8):
        pl.semaphore_signal(
            barrier, inc=1, device_id={"tensor": ((kt + k) % 8) * 2 + core}, device_id_type=MESH
        )
    pl.semaphore_signal(barrier, inc=1, device_id={"tensor": sib}, device_id_type=MESH)
    pl.semaphore_wait(barrier, 11)

    q = core * 8 + kt
    bufs = (tbuf, cbuf)
    srcs = (tok_ref, cot_ref)
    far = [((x + d) % 4) * 2 + yh + flip - 2 * yh * flip for d, flip in HOPS]
    slots = [core * 8 + k for k in far]
    targets = [k * 2 + core for k in far] + [sib]

    def own_copy(g):
        return pltpu.make_async_copy(srcs[g], bufs[g].at[q], loc_sem.at[g])

    def own_send(g, i):
        return ten(srcs[g], bufs[g].at[q], x_send.at[g, i], x_recv.at[g, q], targets[i])

    def pass_on(g, i, slot, dev):
        return ten(bufs[g].at[slot], bufs[g].at[slot], x_send.at[g, i], x_recv.at[g, slot], dev)

    def gather_start(g):
        own_copy(g).start()
        for i in range(8):
            own_send(g, i).start()

    def gather_pair(g):
        for i in ORDER:
            pass_on(g, 0, slots[i], sib).wait_recv()
            pass_on(g, 8 + i, slots[i], sib).start()

    def gather_end(g):
        for k in range(8):
            pass_on(g, 0, (1 - core) * 8 + k, sib).wait_recv()
        own_copy(g).wait()

    gather_start(0)

    common = jnp.int32(EXPERTS - 1)
    for e in range(EXPERTS - 2, -1, -1):
        common = jnp.where(counts_ref[e] == tokens, e, common)
    others = [(common + 1 + j) % EXPERTS for j in range(EXPERTS - 1)]
    ids, cmb = ids_ref[...], comb_ref[...]
    is_c = ids == common
    cc_row = jnp.sum(jnp.where(is_c, cmb, 0.0), 0, keepdims=True)
    co_row = jnp.sum(jnp.where(is_c, 0.0, cmb), 0, keepdims=True)
    id_row = jnp.sum(jnp.where(is_c, 0.0, ids.astype(F32)), 0, keepdims=True)
    which = lax.broadcasted_iota(jnp.int32, (128, tokens), 0)
    grid = jnp.where(which == 0, cc_row, jnp.where(which == 1, co_row, id_row))
    columns = grid.T
    for i in range(16):
        at = (i % 2) * 8 + i // 2
        meta[at * bl : (at + 1) * bl, :] = columns[i * bl : (i + 1) * bl, :]

    gather_pair(0)
    gather_end(0)
    gather_start(1)

    def pair_rows(buf, i):
        return jnp.concatenate([buf[2 * i].astype(F32), buf[2 * i + 1].astype(F32)], 0)

    def prep_x(i, carry):
        rows = pl.ds(pl.multiple_of(i * 2 * bl, 2 * bl), 2 * bl)
        oid = meta[rows, 2:3]
        xv = pair_rows(tbuf, i)
        xs[rows, :] = xv.astype(BF)
        for j, e in enumerate(others):
            xm[j, rows, :] = jnp.where(oid == e.astype(F32), xv, 0.0).astype(BF)
        return carry

    def prep_c(i, carry):
        rows = pl.ds(pl.multiple_of(i * 2 * bl, 2 * bl), 2 * bl)
        m = meta[rows, :]
        cc, co, oid = m[:, 0:1], m[:, 1:2], m[:, 2:3]
        cv = pair_rows(cbuf, i)
        ro = (co * cv).astype(BF).astype(F32)
        rgc[rows, :] = (cc * cv).astype(BF)
        rgo[rows, :] = ro.astype(BF)
        for j, e in enumerate(others):
            rgm[j, rows, :] = jnp.where(oid == e.astype(F32), ro, 0.0).astype(BF)
        for e in range(EXPERTS):
            hit = (oid == float(e)).astype(F32)
            mo[e, rows, :] = jnp.broadcast_to(hit, (2 * bl, fc)).astype(BF)
        cb[0, rows, :] = jnp.broadcast_to(cc, (2 * bl, 256))
        cb[1, rows, :] = jnp.broadcast_to(co, (2 * bl, 256))
        return carry

    lax.fori_loop(0, 8, prep_x, 0)
    for a in range(2):
        for e in range(EXPERTS):
            w_copy(a, e).wait()

    my = pl.ds(pl.multiple_of(yl * half, half), half)
    his = pl.ds(pl.multiple_of((1 - yl) * half, half), half)
    hh = (pl.ds(0, half), pl.ds(half, half))
    qq = (pl.ds(0, quart), pl.ds(quart, quart))
    mq = (
        pl.ds(pl.multiple_of(yl * half, quart), quart),
        pl.ds(pl.multiple_of(yl * half + quart, quart), quart),
    )
    gg = (pl.ds(0, 2), pl.ds(2, 1))

    def by(g, r):
        return sec(pb.at[r, gg[g], his], rby.at[r, gg[g]], b_send.at[g, r], b_recv.at[g, r], yp)

    def ar(g, d):
        return sec(
            pa.at[0, gg[g], hh[d]], rar.at[d, gg[g]], a_send.at[g, d], a_recv.at[g, d], zdev[d]
        )

    def af(g, d, h):
        i = 2 + 2 * d + h
        return sec(
            pa.at[1 + d, gg[g], hh[h]], raf.at[d, gg[g], hh[h]], a_send.at[g, i], a_recv.at[g, i],
            zdev[d],
        )

    def ay(g):
        return sec(sa.at[gg[g]], ray.at[gg[g]], a_send.at[g, 6], a_recv.at[g, 6], yp)

    def br(g, d):
        i = 4 + d
        return sec(
            qb.at[0, gg[g], qq[d]], rbr.at[d, gg[g]], b_send.at[g, i], b_recv.at[g, i], zdev[d]
        )

    def bf(g, d, h):
        i = 6 + 2 * d + h
        return sec(
            qb.at[1 + d, gg[g], qq[h]], rbf.at[d, gg[g], qq[h]], b_send.at[g, i], b_recv.at[g, i],
            zdev[d],
        )

    def chunk_of(r):
        zc = (z + 2 - r + 3 * (r // 2) - 2 * (r // 3)) % NZ
        return pl.ds(pl.multiple_of(zc * fc, fc), fc)

    def leave(g, r):
        @pl.when(r == 0)
        def _():
            ar(g, 0).start()
            ar(g, 1).start()

        @pl.when(r == 1)
        def _():
            af(g, 0, 1).start()

        @pl.when(r == 2)
        def _():
            af(g, 1, 0).start()

    def first_gu(r, carry):
        cols = chunk_of(r)

        def proj_c(a, c2):
            acc = mm(xs[...], wgu[a, common, :, cols])
            paf[r, a] = acc
            pa[r, a] = acc.astype(BF)
            return c2

        lax.fori_loop(0, 2, proj_c, 0)
        leave(0, r)

        def proj_o(a, c2):
            acc = mm(xm[0], wgu[a, others[0], :, cols])
            acc += mm(xm[1], wgu[a, others[1], :, cols])
            acc += mm(xm[2], wgu[a, others[2], :, cols])
            pbf[r, a] = acc
            pb[r, a] = acc.astype(BF)
            return c2

        lax.fori_loop(0, 2, proj_o, 0)
        by(0, r).start()
        return carry

    def first_dh(r, carry):
        cols = chunk_of(r)
        acc = mm_nt(rgc[...], wd[common, cols, :])
        paf[r, 2] = acc
        pa[r, 2] = acc.astype(BF)
        leave(1, r)
        acc = mm_nt(rgm[0], wd[others[0], cols, :])
        acc += mm_nt(rgm[1], wd[others[1], cols, :])
        acc += mm_nt(rgm[2], wd[others[2], cols, :])
        pbf[r, 2] = acc
        pb[r, 2] = acc.astype(BF)
        by(1, r).start()
        return carry

    def a_relay(g):
        for d in (0, 1):
            ar(g, d).wait_recv()
            pa[1 + d, gg[g], hh[d]] = (
                paf[1 + d, gg[g], hh[d]] + rar[d, gg[g]].astype(F32)
            ).astype(BF)
            af(g, d, d).start()

    def a_final(g):
        for d in (0, 1):
            for h in (0, 1):
                af(g, d, h).wait_recv()
        sa[gg[g]] = (
            paf[3, gg[g], his]
            + raf[0, gg[g], his].astype(F32)
            + raf[1, gg[g], his].astype(F32)
        ).astype(BF)
        ay(g).start()

    def b_step(g, r):
        by(g, r).wait_recv()
        if r == 0:
            qb[0, gg[g]] = (pbf[0, gg[g], my] + rby[0, gg[g]].astype(F32)).astype(BF)
            br(g, 0).start()
            br(g, 1).start()
        elif r < 3:
            d = r - 1
            h = 1 - d
            qb[r, gg[g], qq[h]] = (
                pbf[r, gg[g], mq[h]] + rby[r, gg[g], qq[h]].astype(F32)
            ).astype(BF)
            bf(g, d, h).start()
            br(g, d).wait_recv()
            qb[r, gg[g], qq[d]] = (
                pbf[r, gg[g], mq[d]]
                + rby[r, gg[g], qq[d]].astype(F32)
                + rbr[d, gg[g]].astype(F32)
            ).astype(BF)
            bf(g, d, d).start()

    lax.fori_loop(0, NZ, first_gu, 0)
    gather_pair(1)
    a_relay(0)
    b_step(0, 0)
    gather_end(1)
    lax.fori_loop(0, 8, prep_c, 0)
    for e in range(EXPERTS):
        w_copy(2, e).wait()
    lax.fori_loop(0, NZ, first_dh, 0)
    b_step(0, 1)
    b_step(0, 2)
    a_relay(1)
    a_final(0)
    b_step(0, 3)
    b_step(1, 0)
    b_step(1, 1)
    a_final(1)
    b_step(1, 2)
    b_step(1, 3)

    def swiglu(total, dst):
        gate, up, dh = total(0), total(1), total(2)
        sg = 1.0 / (1.0 + jnp.exp(-gate))
        act = gate * sg
        dst[z, 0, my, :] = (act * up).astype(BF)
        dst[z, 1, my, :] = (dh * up * sg * (1.0 + gate * (1.0 - sg))).astype(BF)
        dst[z, 2, my, :] = (dh * act).astype(BF)

    for g in (0, 1):
        for d in (0, 1):
            for h in (0, 1):
                bf(g, d, h).wait_recv()
    swiglu(
        lambda a: pbf[3, a, my, :]
        + rby[3, a].astype(F32)
        + rbf[0, a].astype(F32)
        + rbf[1, a].astype(F32),
        ho,
    )

    z1, z3, z2 = (z + 1) % NZ, (z + 3) % NZ, (z + 2) % NZ

    def oz(zc, d):
        return sec(ho.at[zc, :, my], ho.at[zc, :, my], o_send.at[d], o_recv.at[d], zdev[d])

    def oy(zc, i, rows):
        return sec(ho.at[zc, :, rows], ho.at[zc, :, rows], o_send.at[4 + i], o_recv.at[4 + i], yp)

    def orl(zc, d):
        part = ho.at[zc, :, mq[d]]
        return sec(part, part, o_send.at[2 + d], o_recv.at[2 + d], zdev[d])

    oz(z, 0).start()
    oz(z, 1).start()
    oy(z, 0, my).start()

    ay(0).wait_recv()
    ay(1).wait_recv()
    swiglu(
        lambda a: paf[3, a, my, :]
        + raf[0, a, my, :].astype(F32)
        + raf[1, a, my, :].astype(F32)
        + ray[a].astype(F32),
        hc,
    )

    def cy(rows):
        return sec(hc.at[z, :, rows], hc.at[z, :, rows], c_send.at[0], c_recv.at[0], yp)

    def cz(zc, h, rows, d):
        i = 1 + 2 * d + h
        return sec(hc.at[zc, :, rows], hc.at[zc, :, rows], c_send.at[i], c_recv.at[i], zdev[d])

    def crl(zc, d):
        part = hc.at[zc, :, hh[d]]
        return sec(part, part, c_send.at[5 + d], c_recv.at[5 + d], zdev[d])

    cy(my).start()
    cz(z, yl, my, 0).start()
    cz(z, yl, my, 1).start()

    oz(z3, 0).wait_recv()
    orl(z3, 0).start()
    oy(z3, 1, my).start()
    oz(z1, 1).wait_recv()
    orl(z1, 1).start()
    oy(z1, 2, my).start()
    cy(his).wait_recv()
    cz(z, 1 - yl, his, 0).start()
    cz(z, 1 - yl, his, 1).start()

    xf[...] = jnp.zeros_like(xf)
    cf[...] = jnp.zeros_like(cf)
    for g in (0, 1):
        for r in range(NZ):
            by(g, r).wait_send()

    mine = pl.ds(pl.multiple_of(core * half, half), half)
    theirs = pl.ds(pl.multiple_of((1 - core) * half, half), half)

    def tile(i):
        return pl.ds(pl.multiple_of(i * 256, 256), 256)

    def pair(i):
        return ten(fs.at[i], fr.at[i], p_send.at[i], p_recv.at[i], sib)

    def out_send(i, k):
        return ten(gs.at[i, k], gr.at[i, kt], f_send.at[i, k], f_recv.at[i, kt], k * 2 + core)

    def both(i, k):
        rows = pl.ds(pl.multiple_of(core * half + k * bl, 8), bl)
        return jnp.concatenate([xf[rows, tile(i)], cf[rows, tile(i)]], 0)

    def flush(i):
        pair(i).wait_recv()
        xf[mine, tile(i)] += fr[i, 0].astype(F32)
        cf[mine, tile(i)] += fr[i, 1].astype(F32)

        for d, flip in HOPS:
            k = ((x + d) % 4) * 2 + yh + flip - 2 * yh * flip
            gs[i, k] = both(i, k).astype(BF)
            out_send(i, k).start()

    def second(r, carry):
        zc = (z + 3 * r - 5 * (r // 2) - 2 * (r // 3)) % NZ
        cols = pl.ds(pl.multiple_of(zc * fc, fc), fc)

        @pl.when(r == 1)
        def _():
            for d in (0, 1):
                orl(z2, d).wait_recv()
            oy(z2, 3, my).start()
            cz(z3, 0, hh[0], 0).wait_recv()
            crl(z3, 0).start()
            cz(z1, 1, hh[1], 1).wait_recv()
            crl(z1, 1).start()
            cz(z3, 1, hh[1], 0).wait_recv()

        @pl.when(r == 2)
        def _():
            cz(z1, 0, hh[0], 1).wait_recv()

        @pl.when(r == 3)
        def _():
            crl(z2, 0).wait_recv()
            crl(z2, 1).wait_recv()

        def common_tile(i, c2):
            ns = tile(i)
            xf[:, ns] += cb[0] * mm(hc[zc, 0], wd[common, cols, ns])
            cf[:, ns] += mm_nt(hc[zc, 1], wgu[0, common, ns, cols]) + mm_nt(
                hc[zc, 2], wgu[1, common, ns, cols]
            )
            return c2

        lax.fori_loop(0, nt, common_tile, 0)

        @pl.when(r == 0)
        def _():
            oy(z, 0, his).wait_recv()

        @pl.when(r == 1)
        def _():
            oy(z3, 1, his).wait_recv()

        @pl.when(r == 2)
        def _():
            oy(z1, 2, his).wait_recv()

        @pl.when(r == 3)
        def _():
            oy(z2, 3, his).wait_recv()

        for j, e in enumerate(others):
            hit = mo[e]
            for a in range(3):
                pb[j, a] = ho[zc, a] * hit

        def other_tile(i, c2):
            ns = tile(i)
            acc = mm(pb[0, 0], wd[others[0], cols, ns])
            acc += mm(pb[1, 0], wd[others[1], cols, ns])
            acc += mm(pb[2, 0], wd[others[2], cols, ns])
            xf[:, ns] += cb[1] * acc
            acc = mm_nt(pb[0, 1], wgu[0, others[0], ns, cols])
            acc += mm_nt(pb[0, 2], wgu[1, others[0], ns, cols])
            for j in (1, 2):
                acc += mm_nt(pb[j, 1], wgu[0, others[j], ns, cols])
                acc += mm_nt(pb[j, 2], wgu[1, others[j], ns, cols])
            cf[:, ns] += acc

            @pl.when(r == 3)
            def _():
                fs[i, 0] = xf[theirs, ns].astype(BF)
                fs[i, 1] = cf[theirs, ns].astype(BF)
                pair(i).start()

                @pl.when(i > 0)
                def _():
                    flush(i - 1)

            return c2

        lax.fori_loop(0, nt, other_tile, 0)
        return carry

    lax.fori_loop(0, NZ, second, 0)
    flush(nt - 1)

    def weight_grad(e, carry):
        here = (common == e).astype(F32)
        mc = here.astype(BF)
        hit = mo[e]
        xs[...] = rgc[...] * mc + rgo[...] * (1.0 - here).astype(BF)

        def block(zc, c2):
            hs = hc[zc, 0] * mc + ho[zc, 0] * hit
            rows = pl.ds(pl.multiple_of(zc * fc, fc), fc)
            for i in range(nt):
                ns = pl.ds(i * 256, 256)
                dd_ref[e, rows, ns] = mm_tn(hs, xs[:, ns]).astype(BF)
            return c2

        lax.fori_loop(0, NZ, block, 0)
        return carry

    lax.fori_loop(0, EXPERTS, weight_grad, 0)

    for i in range(nt):
        total = both(i, kt)
        for n in range(1, 8):
            k = (kt + n) % 8
            dev = k * 2 + core
            ten(gs.at[i, k], gr.at[i, k], f_send.at[i, k], f_recv.at[i, k], dev).wait_recv()
            total += gr[i, k].astype(F32)
        lo_ref[:, i * 256 : (i + 1) * 256] = total[:bl].astype(BF)
        dt_ref[:, i * 256 : (i + 1) * 256] = total[bl:].astype(BF)

    for i in range(nt):
        pair(i).wait_send()
        for n in range(1, 8):
            out_send(i, (kt + n) % 8).wait_send()
    for g in (0, 1):
        for i in range(8):
            own_send(g, i).wait_send()
        for i in range(7):
            pass_on(g, 8 + i, slots[i], sib).wait_send()
        for d in (0, 1):
            ar(g, d).wait_send()
            br(g, d).wait_send()
            for h in (0, 1):
                af(g, d, h).wait_send()
                bf(g, d, h).wait_send()
        ay(g).wait_send()
    for d, zc in ((0, z3), (1, z1)):
        oz(z, d).wait_send()
        orl(zc, d).wait_send()
        crl(zc, d).wait_send()
        cz(z, yl, my, d).wait_send()
        cz(z, 1 - yl, his, d).wait_send()
    for i, zc in enumerate((z, z3, z1, z2)):
        oy(zc, i, my).wait_send()
    cy(my).wait_send()


def on_device(tokens, combine, expert_ids, expert_counts, w_gate, w_up, w_down, cotangent):
    total = combine.shape[0]
    bl, dloc = tokens.shape
    floc = w_gate.shape[2]
    fc = floc // NZ
    half, quart = total // 2, total // 4
    nt = dloc // 256
    any_spec = pl.BlockSpec(memory_space=pl.ANY)
    vmem = pl.BlockSpec(memory_space=pltpu.VMEM)
    V = pltpu.VMEM
    dma = pltpu.SemaphoreType.DMA
    return pl.pallas_call(
        layer_kernel,
        out_shape=(V((bl, dloc), BF), V((bl, dloc), BF), V((EXPERTS, floc, dloc), BF)),
        in_specs=[pl.BlockSpec(memory_space=pltpu.SMEM)] + [vmem] * 4 + [any_spec] * 3,
        out_specs=(vmem, vmem, vmem),
        scratch_shapes=[
            V((2, EXPERTS, dloc, floc), BF),
            V((EXPERTS, floc, dloc), BF),
            V((16, bl, dloc), BF),
            V((16, bl, dloc), BF),
            V((total, 128), F32),
            V((total, dloc), F32),
            V((total, dloc), F32),
            V((total, dloc), BF),
            V((EXPERTS - 1, total, dloc), BF),
            V((total, dloc), BF),
            V((total, dloc), BF),
            V((EXPERTS - 1, total, dloc), BF),
            V((EXPERTS, total, fc), BF),
            V((2, total, 256), F32),
            V((NZ, 3, total, fc), BF),
            V((NZ, 3, total, fc), F32),
            V((NZ, 3, total, fc), BF),
            V((NZ, 3, total, fc), F32),
            V((2, 3, half, fc), BF),
            V((2, 3, total, fc), BF),
            V((3, half, fc), BF),
            V((3, half, fc), BF),
            V((NZ, 3, half, fc), BF),
            V((3, 3, half, fc), BF),
            V((2, 3, quart, fc), BF),
            V((2, 3, half, fc), BF),
            V((NZ, 3, total, fc), BF),
            V((NZ, 3, total, fc), BF),
            V((nt, 2, half, 256), BF),
            V((nt, 2, half, 256), BF),
            V((nt, 8, 2 * bl, 256), BF),
            V((nt, 8, 2 * bl, 256), BF),
            dma((3, EXPERTS)),
            dma((2,)),
            dma((2, 15)),
            dma((2, 16)),
            dma((2, 7)),
            dma((2, 7)),
            dma((2, 10)),
            dma((2, 10)),
            dma((7,)),
            dma((7,)),
            dma((8,)),
            dma((8,)),
            dma((nt,)),
            dma((nt,)),
            dma((nt, 8)),
            dma((nt, 8)),
        ],
        compiler_params=pltpu.CompilerParams(
            collective_id=0, has_side_effects=True, vmem_limit_bytes=VLIM
        ),
    )(expert_counts, combine.T, expert_ids.T, tokens, cotangent, w_gate, w_up, w_down)


def solution(mesh):
    in_specs = (
        P("tensor", "section"),
        P(),
        P(),
        P(),
        P(None, "section", "tensor"),
        P(None, "section", "tensor"),
        P(None, "tensor", "section"),
        P("tensor", "section"),
    )
    out_specs = (P("tensor", "section"), P("tensor", "section"), P(None, "tensor", "section"))
    return jax.shard_map(
        on_device, mesh=mesh, in_specs=in_specs, out_specs=out_specs, check_vma=False
    )
```

```python
import jax
import jax.numpy as jnp
from jax import lax
from jax.experimental import pallas as pl
from jax.experimental.pallas import tpu as pltpu
from jax.sharding import PartitionSpec as P

EXPERTS = 4
NZ = 4
VLIM = 60000000
HOPS = ((2, 1), (1, 1), (3, 1), (0, 1), (2, 0), (1, 0), (3, 0))
ORDER = (5, 6, 4, 3, 1, 2, 0)
BF = jnp.bfloat16
F32 = jnp.float32
MESH = pl.DeviceIdType.MESH


def mm(a, b):
    return jnp.dot(a, b, preferred_element_type=F32)


def mm_nt(a, b):
    return lax.dot_general(a, b, (((1,), (1,)), ((), ())), preferred_element_type=F32)


def mm_tn(a, b):
    return lax.dot_general(a, b, (((0,), (0,)), ((), ())), preferred_element_type=F32)


def layer_kernel(
    counts_ref, comb_ref, ids_ref, tok_ref, cot_ref, wg_hbm, wu_hbm, wd_hbm,
    lo_ref, dt_ref, dd_ref,
    wgu, wd, tbuf, cbuf, meta, xf, cf, xs, xm, rgc, rgo, rgm, mo, cb,
    pa, paf, pb, pbf, rar, raf, sa, ray, rby, qb, rbr, rbf, hc, ho, fs, fr, gs, gr,
    w_sem, loc_sem, x_send, x_recv, a_send, a_recv, b_send, b_recv,
    c_send, c_recv, o_send, o_recv, p_send, p_recv, f_send, f_recv,
):
    tokens, dloc = xf.shape
    fc = pa.shape[-1]
    half = tokens // 2
    quart = half // 2
    bl = tokens // 16
    nt = dloc // 256

    s = lax.axis_index("section")
    t = lax.axis_index("tensor")
    z, yl = s // 2, s % 2
    zp = ((z + 1) % NZ) * 2 + yl
    zm = ((z + 3) % NZ) * 2 + yl
    yp = z * 2 + 1 - yl
    zdev = (zp, zm)
    core, kt, x = t % 2, t // 2, t // 4
    yh = kt % 2

    def tx(d):
        return ((x + d) % 4) * 4 + yh * 2 + core

    ty = x * 4 + (1 - yh) * 2 + core
    sib = t + 1 - 2 * core

    def sec(src, dst, ssem, rsem, dev):
        return pltpu.make_async_remote_copy(src, dst, ssem, rsem, {"section": dev}, MESH)

    def ten(src, dst, ssem, rsem, dev):
        return pltpu.make_async_remote_copy(src, dst, ssem, rsem, {"tensor": dev}, MESH)

    def w_copy(a, e):
        if a == 2:
            return pltpu.make_async_copy(wd_hbm.at[e], wd.at[e], w_sem.at[2, e])
        return pltpu.make_async_copy((wg_hbm, wu_hbm)[a].at[e], wgu.at[a, e], w_sem.at[a, e])

    for a in range(3):
        for e in range(EXPERTS):
            w_copy(a, e).start()

    barrier = pltpu.get_barrier_semaphore()
    for dev in (zp, zm, yp):
        pl.semaphore_signal(barrier, inc=1, device_id={"section": dev}, device_id_type=MESH)
    for k in range(1, 8):
        pl.semaphore_signal(
            barrier, inc=1, device_id={"tensor": ((kt + k) % 8) * 2 + core}, device_id_type=MESH
        )
    pl.semaphore_signal(barrier, inc=1, device_id={"tensor": sib}, device_id_type=MESH)
    pl.semaphore_wait(barrier, 11)

    q = core * 8 + kt
    bufs = (tbuf, cbuf)
    srcs = (tok_ref, cot_ref)
    far = [((x + d) % 4) * 2 + yh + flip - 2 * yh * flip for d, flip in HOPS]
    slots = [core * 8 + k for k in far]
    targets = [k * 2 + core for k in far] + [sib]

    def own_copy(g):
        return pltpu.make_async_copy(srcs[g], bufs[g].at[q], loc_sem.at[g])

    def own_send(g, i):
        return ten(srcs[g], bufs[g].at[q], x_send.at[g, i], x_recv.at[g, q], targets[i])

    def pass_on(g, i, slot, dev):
        return ten(bufs[g].at[slot], bufs[g].at[slot], x_send.at[g, i], x_recv.at[g, slot], dev)

    def gather_start(g):
        own_copy(g).start()
        for i in range(8):
            own_send(g, i).start()

    def gather_pair(g):
        for i in ORDER:
            pass_on(g, 0, slots[i], sib).wait_recv()
            pass_on(g, 8 + i, slots[i], sib).start()

    def gather_end(g):
        for k in range(8):
            pass_on(g, 0, (1 - core) * 8 + k, sib).wait_recv()
        own_copy(g).wait()

    gather_start(0)

    common = jnp.int32(EXPERTS - 1)
    for e in range(EXPERTS - 2, -1, -1):
        common = jnp.where(counts_ref[e] == tokens, e, common)
    others = [(common + 1 + j) % EXPERTS for j in range(EXPERTS - 1)]
    ids, cmb = ids_ref[...], comb_ref[...]
    is_c = ids == common
    cc_row = jnp.sum(jnp.where(is_c, cmb, 0.0), 0, keepdims=True)
    co_row = jnp.sum(jnp.where(is_c, 0.0, cmb), 0, keepdims=True)
    id_row = jnp.sum(jnp.where(is_c, 0.0, ids.astype(F32)), 0, keepdims=True)
    which = lax.broadcasted_iota(jnp.int32, (128, tokens), 0)
    grid = jnp.where(which == 0, cc_row, jnp.where(which == 1, co_row, id_row))
    columns = grid.T
    for i in range(16):
        at = (i % 2) * 8 + i // 2
        meta[at * bl : (at + 1) * bl, :] = columns[i * bl : (i + 1) * bl, :]

    gather_pair(0)
    gather_end(0)
    gather_start(1)

    def pair_rows(buf, i):
        return jnp.concatenate([buf[2 * i].astype(F32), buf[2 * i + 1].astype(F32)], 0)

    def prep_x(i, carry):
        rows = pl.ds(pl.multiple_of(i * 2 * bl, 2 * bl), 2 * bl)
        oid = meta[rows, 2:3]
        xv = pair_rows(tbuf, i)
        xs[rows, :] = xv.astype(BF)
        for j, e in enumerate(others):
            xm[j, rows, :] = jnp.where(oid == e.astype(F32), xv, 0.0).astype(BF)
        return carry

    def prep_c(i, carry):
        rows = pl.ds(pl.multiple_of(i * 2 * bl, 2 * bl), 2 * bl)
        m = meta[rows, :]
        cc, co, oid = m[:, 0:1], m[:, 1:2], m[:, 2:3]
        cv = pair_rows(cbuf, i)
        ro = (co * cv).astype(BF).astype(F32)
        rgc[rows, :] = (cc * cv).astype(BF)
        rgo[rows, :] = ro.astype(BF)
        for j, e in enumerate(others):
            rgm[j, rows, :] = jnp.where(oid == e.astype(F32), ro, 0.0).astype(BF)
        for e in range(EXPERTS):
            hit = (oid == float(e)).astype(F32)
            mo[e, rows, :] = jnp.broadcast_to(hit, (2 * bl, fc)).astype(BF)
        cb[0, rows, :] = jnp.broadcast_to(cc, (2 * bl, 256))
        cb[1, rows, :] = jnp.broadcast_to(co, (2 * bl, 256))
        return carry

    lax.fori_loop(0, 8, prep_x, 0)
    for a in range(2):
        for e in range(EXPERTS):
            w_copy(a, e).wait()

    my = pl.ds(pl.multiple_of(yl * half, half), half)
    his = pl.ds(pl.multiple_of((1 - yl) * half, half), half)
    hh = (pl.ds(0, half), pl.ds(half, half))
    qq = (pl.ds(0, quart), pl.ds(quart, quart))
    mq = (
        pl.ds(pl.multiple_of(yl * half, quart), quart),
        pl.ds(pl.multiple_of(yl * half + quart, quart), quart),
    )
    gg = (pl.ds(0, 2), pl.ds(2, 1))

    def by(g, r):
        return sec(pb.at[r, gg[g], his], rby.at[r, gg[g]], b_send.at[g, r], b_recv.at[g, r], yp)

    def ar(g, d):
        return sec(
            pa.at[0, gg[g], hh[d]], rar.at[d, gg[g]], a_send.at[g, d], a_recv.at[g, d], zdev[d]
        )

    def af(g, d, h):
        i = 2 + 2 * d + h
        return sec(
            pa.at[1 + d, gg[g], hh[h]], raf.at[d, gg[g], hh[h]], a_send.at[g, i], a_recv.at[g, i],
            zdev[d],
        )

    def ay(g):
        return sec(sa.at[gg[g]], ray.at[gg[g]], a_send.at[g, 6], a_recv.at[g, 6], yp)

    def br(g, d):
        i = 4 + d
        return sec(
            qb.at[0, gg[g], qq[d]], rbr.at[d, gg[g]], b_send.at[g, i], b_recv.at[g, i], zdev[d]
        )

    def bf(g, d, h):
        i = 6 + 2 * d + h
        return sec(
            qb.at[1 + d, gg[g], qq[h]], rbf.at[d, gg[g], qq[h]], b_send.at[g, i], b_recv.at[g, i],
            zdev[d],
        )

    def chunk_of(r):
        zc = (z + 2 - r + 3 * (r // 2) - 2 * (r // 3)) % NZ
        return pl.ds(pl.multiple_of(zc * fc, fc), fc)

    def leave(g, r):
        @pl.when(r == 0)
        def _():
            ar(g, 0).start()
            ar(g, 1).start()

        @pl.when(r == 1)
        def _():
            af(g, 0, 1).start()

        @pl.when(r == 2)
        def _():
            af(g, 1, 0).start()

    def first_gu(r, carry):
        cols = chunk_of(r)

        def proj_c(a, c2):
            acc = mm(xs[...], wgu[a, common, :, cols])
            paf[r, a] = acc
            pa[r, a] = acc.astype(BF)
            return c2

        lax.fori_loop(0, 2, proj_c, 0)
        leave(0, r)

        def proj_o(a, c2):
            acc = mm(xm[0], wgu[a, others[0], :, cols])
            acc += mm(xm[1], wgu[a, others[1], :, cols])
            acc += mm(xm[2], wgu[a, others[2], :, cols])
            pbf[r, a] = acc
            pb[r, a] = acc.astype(BF)
            return c2

        lax.fori_loop(0, 2, proj_o, 0)
        by(0, r).start()
        return carry

    def first_dh(r, carry):
        cols = chunk_of(r)

        @pl.when(r == 2)
        def _():
            b_step(0, 1)

        acc = mm_nt(rgc[...], wd[common, cols, :])
        paf[r, 2] = acc
        pa[r, 2] = acc.astype(BF)
        leave(1, r)
        acc = mm_nt(rgm[0], wd[others[0], cols, :])
        acc += mm_nt(rgm[1], wd[others[1], cols, :])
        acc += mm_nt(rgm[2], wd[others[2], cols, :])
        pbf[r, 2] = acc
        pb[r, 2] = acc.astype(BF)
        by(1, r).start()
        return carry

    def a_relay(g):
        for d in (0, 1):
            ar(g, d).wait_recv()
            pa[1 + d, gg[g], hh[d]] = (
                paf[1 + d, gg[g], hh[d]] + rar[d, gg[g]].astype(F32)
            ).astype(BF)
            af(g, d, d).start()

    def a_final(g):
        for d in (0, 1):
            for h in (0, 1):
                af(g, d, h).wait_recv()
        sa[gg[g]] = (
            paf[3, gg[g], his]
            + raf[0, gg[g], his].astype(F32)
            + raf[1, gg[g], his].astype(F32)
        ).astype(BF)
        ay(g).start()

    def b_step(g, r):
        by(g, r).wait_recv()
        if r == 0:
            qb[0, gg[g]] = (pbf[0, gg[g], my] + rby[0, gg[g]].astype(F32)).astype(BF)
            br(g, 0).start()
            br(g, 1).start()
        elif r < 3:
            d = r - 1
            h = 1 - d
            qb[r, gg[g], qq[h]] = (
                pbf[r, gg[g], mq[h]] + rby[r, gg[g], qq[h]].astype(F32)
            ).astype(BF)
            bf(g, d, h).start()
            br(g, d).wait_recv()
            qb[r, gg[g], qq[d]] = (
                pbf[r, gg[g], mq[d]]
                + rby[r, gg[g], qq[d]].astype(F32)
                + rbr[d, gg[g]].astype(F32)
            ).astype(BF)
            bf(g, d, d).start()

    lax.fori_loop(0, NZ, first_gu, 0)
    gather_pair(1)
    a_relay(0)
    b_step(0, 0)
    gather_end(1)
    lax.fori_loop(0, 8, prep_c, 0)
    for e in range(EXPERTS):
        w_copy(2, e).wait()
    lax.fori_loop(0, NZ, first_dh, 0)
    b_step(0, 2)
    a_relay(1)
    a_final(0)
    b_step(0, 3)
    b_step(1, 0)
    b_step(1, 1)
    a_final(1)
    b_step(1, 2)
    b_step(1, 3)

    def swiglu(total, dst):
        gate, up, dh = total(0), total(1), total(2)
        sg = 1.0 / (1.0 + jnp.exp(-gate))
        act = gate * sg
        dst[z, 0, my, :] = (act * up).astype(BF)
        dst[z, 1, my, :] = (dh * up * sg * (1.0 + gate * (1.0 - sg))).astype(BF)
        dst[z, 2, my, :] = (dh * act).astype(BF)

    for g in (0, 1):
        for d in (0, 1):
            for h in (0, 1):
                bf(g, d, h).wait_recv()
    swiglu(
        lambda a: pbf[3, a, my, :]
        + rby[3, a].astype(F32)
        + rbf[0, a].astype(F32)
        + rbf[1, a].astype(F32),
        ho,
    )

    z1, z3, z2 = (z + 1) % NZ, (z + 3) % NZ, (z + 2) % NZ

    def oz(zc, d):
        return sec(ho.at[zc, :, my], ho.at[zc, :, my], o_send.at[d], o_recv.at[d], zdev[d])

    def oy(zc, i, rows):
        return sec(ho.at[zc, :, rows], ho.at[zc, :, rows], o_send.at[4 + i], o_recv.at[4 + i], yp)

    def orl(zc, d):
        part = ho.at[zc, :, mq[d]]
        return sec(part, part, o_send.at[2 + d], o_recv.at[2 + d], zdev[d])

    oz(z, 0).start()
    oz(z, 1).start()
    oy(z, 0, my).start()

    ay(0).wait_recv()
    ay(1).wait_recv()
    swiglu(
        lambda a: paf[3, a, my, :]
        + raf[0, a, my, :].astype(F32)
        + raf[1, a, my, :].astype(F32)
        + ray[a].astype(F32),
        hc,
    )

    def cy(rows):
        return sec(hc.at[z, :, rows], hc.at[z, :, rows], c_send.at[0], c_recv.at[0], yp)

    def cz(zc, h, rows, d):
        i = 1 + 2 * d + h
        return sec(hc.at[zc, :, rows], hc.at[zc, :, rows], c_send.at[i], c_recv.at[i], zdev[d])

    def crl(zc, d):
        part = hc.at[zc, :, hh[d]]
        return sec(part, part, c_send.at[5 + d], c_recv.at[5 + d], zdev[d])

    cy(my).start()
    cz(z, yl, my, 0).start()
    cz(z, yl, my, 1).start()

    oz(z3, 0).wait_recv()
    orl(z3, 0).start()
    oy(z3, 1, my).start()
    oz(z1, 1).wait_recv()
    orl(z1, 1).start()
    oy(z1, 2, my).start()
    cy(his).wait_recv()
    cz(z, 1 - yl, his, 0).start()
    cz(z, 1 - yl, his, 1).start()

    xf[...] = jnp.zeros_like(xf)
    cf[...] = jnp.zeros_like(cf)
    for g in (0, 1):
        for r in range(NZ):
            by(g, r).wait_send()

    mine = pl.ds(pl.multiple_of(core * half, half), half)
    theirs = pl.ds(pl.multiple_of((1 - core) * half, half), half)

    def tile(i):
        return pl.ds(pl.multiple_of(i * 256, 256), 256)

    def pair(i):
        return ten(fs.at[i], fr.at[i], p_send.at[i], p_recv.at[i], sib)

    def out_send(i, k):
        return ten(gs.at[i, k], gr.at[i, kt], f_send.at[i, k], f_recv.at[i, kt], k * 2 + core)

    def both(i, k):
        rows = pl.ds(pl.multiple_of(core * half + k * bl, 8), bl)
        return jnp.concatenate([xf[rows, tile(i)], cf[rows, tile(i)]], 0)

    def flush(i):
        pair(i).wait_recv()
        xf[mine, tile(i)] += fr[i, 0].astype(F32)
        cf[mine, tile(i)] += fr[i, 1].astype(F32)

        for d, flip in HOPS:
            k = ((x + d) % 4) * 2 + yh + flip - 2 * yh * flip
            gs[i, k] = both(i, k).astype(BF)
            out_send(i, k).start()

    def second(r, carry):
        zc = (z + 3 * r - 5 * (r // 2) - 2 * (r // 3)) % NZ
        cols = pl.ds(pl.multiple_of(zc * fc, fc), fc)

        @pl.when(r == 1)
        def _():
            for d in (0, 1):
                orl(z2, d).wait_recv()
            oy(z2, 3, my).start()
            cz(z3, 0, hh[0], 0).wait_recv()
            crl(z3, 0).start()
            cz(z1, 1, hh[1], 1).wait_recv()
            crl(z1, 1).start()
            cz(z3, 1, hh[1], 0).wait_recv()

        @pl.when(r == 2)
        def _():
            cz(z1, 0, hh[0], 1).wait_recv()

        @pl.when(r == 3)
        def _():
            crl(z2, 0).wait_recv()
            crl(z2, 1).wait_recv()

        def common_tile(i, c2):
            ns = tile(i)
            xf[:, ns] += cb[0] * mm(hc[zc, 0], wd[common, cols, ns])
            cf[:, ns] += mm_nt(hc[zc, 1], wgu[0, common, ns, cols]) + mm_nt(
                hc[zc, 2], wgu[1, common, ns, cols]
            )
            return c2

        lax.fori_loop(0, nt, common_tile, 0)

        @pl.when(r == 0)
        def _():
            oy(z, 0, his).wait_recv()

        @pl.when(r == 1)
        def _():
            oy(z3, 1, his).wait_recv()

        @pl.when(r == 2)
        def _():
            oy(z1, 2, his).wait_recv()

        @pl.when(r == 3)
        def _():
            oy(z2, 3, his).wait_recv()

        for j, e in enumerate(others):
            hit = mo[e]
            for a in range(3):
                pb[j, a] = ho[zc, a] * hit

        def other_tile(i, c2):
            ns = tile(i)
            acc = mm(pb[0, 0], wd[others[0], cols, ns])
            acc += mm(pb[1, 0], wd[others[1], cols, ns])
            acc += mm(pb[2, 0], wd[others[2], cols, ns])
            xf[:, ns] += cb[1] * acc
            acc = mm_nt(pb[0, 1], wgu[0, others[0], ns, cols])
            acc += mm_nt(pb[0, 2], wgu[1, others[0], ns, cols])
            for j in (1, 2):
                acc += mm_nt(pb[j, 1], wgu[0, others[j], ns, cols])
                acc += mm_nt(pb[j, 2], wgu[1, others[j], ns, cols])
            cf[:, ns] += acc

            @pl.when(r == 3)
            def _():
                fs[i, 0] = xf[theirs, ns].astype(BF)
                fs[i, 1] = cf[theirs, ns].astype(BF)
                pair(i).start()

            return c2

        lax.fori_loop(0, nt, other_tile, 0)
        return carry

    lax.fori_loop(0, NZ, second, 0)
    for i in range(nt):
        flush(i)

    def weight_grad(e, carry):
        here = (common == e).astype(F32)
        mc = here.astype(BF)
        hit = mo[e]
        xs[...] = rgc[...] * mc + rgo[...] * (1.0 - here).astype(BF)

        def block(zc, c2):
            hs = hc[zc, 0] * mc + ho[zc, 0] * hit
            rows = pl.ds(pl.multiple_of(zc * fc, fc), fc)
            for i in range(nt):
                ns = pl.ds(i * 256, 256)
                dd_ref[e, rows, ns] = mm_tn(hs, xs[:, ns]).astype(BF)
            return c2

        lax.fori_loop(0, NZ, block, 0)
        return carry

    lax.fori_loop(0, EXPERTS, weight_grad, 0)

    for i in range(nt):
        total = both(i, kt)
        for n in range(1, 8):
            k = (kt + n) % 8
            dev = k * 2 + core
            ten(gs.at[i, k], gr.at[i, k], f_send.at[i, k], f_recv.at[i, k], dev).wait_recv()
            total += gr[i, k].astype(F32)
        lo_ref[:, i * 256 : (i + 1) * 256] = total[:bl].astype(BF)
        dt_ref[:, i * 256 : (i + 1) * 256] = total[bl:].astype(BF)

    for i in range(nt):
        pair(i).wait_send()
        for n in range(1, 8):
            out_send(i, (kt + n) % 8).wait_send()
    for g in (0, 1):
        for i in range(8):
            own_send(g, i).wait_send()
        for i in range(7):
            pass_on(g, 8 + i, slots[i], sib).wait_send()
        for d in (0, 1):
            ar(g, d).wait_send()
            br(g, d).wait_send()
            for h in (0, 1):
                af(g, d, h).wait_send()
                bf(g, d, h).wait_send()
        ay(g).wait_send()
    for d, zc in ((0, z3), (1, z1)):
        oz(z, d).wait_send()
        orl(zc, d).wait_send()
        crl(zc, d).wait_send()
        cz(z, yl, my, d).wait_send()
        cz(z, 1 - yl, his, d).wait_send()
    for i, zc in enumerate((z, z3, z1, z2)):
        oy(zc, i, my).wait_send()
    cy(my).wait_send()


def on_device(tokens, combine, expert_ids, expert_counts, w_gate, w_up, w_down, cotangent):
    total = combine.shape[0]
    bl, dloc = tokens.shape
    floc = w_gate.shape[2]
    fc = floc // NZ
    half, quart = total // 2, total // 4
    nt = dloc // 256
    any_spec = pl.BlockSpec(memory_space=pl.ANY)
    vmem = pl.BlockSpec(memory_space=pltpu.VMEM)
    V = pltpu.VMEM
    dma = pltpu.SemaphoreType.DMA
    return pl.pallas_call(
        layer_kernel,
        out_shape=(V((bl, dloc), BF), V((bl, dloc), BF), V((EXPERTS, floc, dloc), BF)),
        in_specs=[pl.BlockSpec(memory_space=pltpu.SMEM)] + [vmem] * 4 + [any_spec] * 3,
        out_specs=(vmem, vmem, vmem),
        scratch_shapes=[
            V((2, EXPERTS, dloc, floc), BF),
            V((EXPERTS, floc, dloc), BF),
            V((16, bl, dloc), BF),
            V((16, bl, dloc), BF),
            V((total, 128), F32),
            V((total, dloc), F32),
            V((total, dloc), F32),
            V((total, dloc), BF),
            V((EXPERTS - 1, total, dloc), BF),
            V((total, dloc), BF),
            V((total, dloc), BF),
            V((EXPERTS - 1, total, dloc), BF),
            V((EXPERTS, total, fc), BF),
            V((2, total, 256), F32),
            V((NZ, 3, total, fc), BF),
            V((NZ, 3, total, fc), F32),
            V((NZ, 3, total, fc), BF),
            V((NZ, 3, total, fc), F32),
            V((2, 3, half, fc), BF),
            V((2, 3, total, fc), BF),
            V((3, half, fc), BF),
            V((3, half, fc), BF),
            V((NZ, 3, half, fc), BF),
            V((3, 3, half, fc), BF),
            V((2, 3, quart, fc), BF),
            V((2, 3, half, fc), BF),
            V((NZ, 3, total, fc), BF),
            V((NZ, 3, total, fc), BF),
            V((nt, 2, half, 256), BF),
            V((nt, 2, half, 256), BF),
            V((nt, 8, 2 * bl, 256), BF),
            V((nt, 8, 2 * bl, 256), BF),
            dma((3, EXPERTS)),
            dma((2,)),
            dma((2, 15)),
            dma((2, 16)),
            dma((2, 7)),
            dma((2, 7)),
            dma((2, 10)),
            dma((2, 10)),
            dma((7,)),
            dma((7,)),
            dma((8,)),
            dma((8,)),
            dma((nt,)),
            dma((nt,)),
            dma((nt, 8)),
            dma((nt, 8)),
        ],
        compiler_params=pltpu.CompilerParams(
            collective_id=0, has_side_effects=True, vmem_limit_bytes=VLIM
        ),
    )(expert_counts, combine.T, expert_ids.T, tokens, cotangent, w_gate, w_up, w_down)


def solution(mesh):
    in_specs = (
        P("tensor", "section"),
        P(),
        P(),
        P(),
        P(None, "section", "tensor"),
        P(None, "section", "tensor"),
        P(None, "tensor", "section"),
        P("tensor", "section"),
    )
    out_specs = (P("tensor", "section"), P("tensor", "section"), P(None, "tensor", "section"))
    return jax.shard_map(
        on_device, mesh=mesh, in_specs=in_specs, out_specs=out_specs, check_vma=False
    )
```

```python
import jax
import jax.numpy as jnp
from jax import lax
from jax.experimental import pallas as pl
from jax.experimental.pallas import tpu as pltpu
from jax.sharding import PartitionSpec as P

EXPERTS = 4
NZ = 4
VLIM = 60000000
HOPS = ((2, 1), (1, 1), (3, 1), (0, 1), (2, 0), (1, 0), (3, 0))
ORDER = (5, 6, 4, 3, 1, 2, 0)
BF = jnp.bfloat16
F32 = jnp.float32
MESH = pl.DeviceIdType.MESH


def mm(a, b):
    return jnp.dot(a, b, preferred_element_type=F32)


def mm_nt(a, b):
    return lax.dot_general(a, b, (((1,), (1,)), ((), ())), preferred_element_type=F32)


def mm_tn(a, b):
    return lax.dot_general(a, b, (((0,), (0,)), ((), ())), preferred_element_type=F32)


def layer_kernel(
    counts_ref, comb_ref, ids_ref, tok_ref, cot_ref, wg_hbm, wu_hbm, wd_hbm,
    lo_ref, dt_ref, dd_ref,
    wgu, wd, tbuf, cbuf, meta, xf, cf, xs, xm, rgc, rgo, rgm, mo, cb,
    pa, paf, pb, pbf, rar, raf, sa, ray, rby, qb, rbr, rbf, hc, ho, fs, fr, gs, gr,
    w_sem, loc_sem, x_send, x_recv, a_send, a_recv, b_send, b_recv,
    c_send, c_recv, o_send, o_recv, p_send, p_recv, f_send, f_recv,
):
    tokens, dloc = xf.shape
    fc = pa.shape[-1]
    half = tokens // 2
    quart = half // 2
    bl = tokens // 16
    nt = dloc // 256

    s = lax.axis_index("section")
    t = lax.axis_index("tensor")
    z, yl = s // 2, s % 2
    zp = ((z + 1) % NZ) * 2 + yl
    zm = ((z + 3) % NZ) * 2 + yl
    yp = z * 2 + 1 - yl
    zdev = (zp, zm)
    core, kt, x = t % 2, t // 2, t // 4
    yh = kt % 2

    def tx(d):
        return ((x + d) % 4) * 4 + yh * 2 + core

    ty = x * 4 + (1 - yh) * 2 + core
    sib = t + 1 - 2 * core

    def sec(src, dst, ssem, rsem, dev):
        return pltpu.make_async_remote_copy(src, dst, ssem, rsem, {"section": dev}, MESH)

    def ten(src, dst, ssem, rsem, dev):
        return pltpu.make_async_remote_copy(src, dst, ssem, rsem, {"tensor": dev}, MESH)

    def w_copy(a, e):
        if a == 2:
            return pltpu.make_async_copy(wd_hbm.at[e], wd.at[e], w_sem.at[2, e])
        return pltpu.make_async_copy((wg_hbm, wu_hbm)[a].at[e], wgu.at[a, e], w_sem.at[a, e])

    for a in range(3):
        for e in range(EXPERTS):
            w_copy(a, e).start()

    barrier = pltpu.get_barrier_semaphore()
    for dev in (zp, zm, yp):
        pl.semaphore_signal(barrier, inc=1, device_id={"section": dev}, device_id_type=MESH)
    for k in range(1, 8):
        pl.semaphore_signal(
            barrier, inc=1, device_id={"tensor": ((kt + k) % 8) * 2 + core}, device_id_type=MESH
        )
    pl.semaphore_signal(barrier, inc=1, device_id={"tensor": sib}, device_id_type=MESH)
    pl.semaphore_wait(barrier, 11)

    q = core * 8 + kt
    bufs = (tbuf, cbuf)
    srcs = (tok_ref, cot_ref)
    far = [((x + d) % 4) * 2 + yh + flip - 2 * yh * flip for d, flip in HOPS]
    slots = [core * 8 + k for k in far]
    targets = [k * 2 + core for k in far] + [sib]

    def own_copy(g):
        return pltpu.make_async_copy(srcs[g], bufs[g].at[q], loc_sem.at[g])

    def own_send(g, i):
        return ten(srcs[g], bufs[g].at[q], x_send.at[g, i], x_recv.at[g, q], targets[i])

    def pass_on(g, i, slot, dev):
        return ten(bufs[g].at[slot], bufs[g].at[slot], x_send.at[g, i], x_recv.at[g, slot], dev)

    def gather_start(g):
        own_copy(g).start()
        for i in range(8) if g == 0 else (3, 4, 5, 6, 7):
            own_send(g, i).start()

    def gather_mid():
        pass_on(1, 0, slots[3], sib).wait_recv()
        for i in range(3):
            pass_on(1, i, slots[3], targets[4 + i]).start()
        pass_on(1, 8 + 3, slots[3], sib).start()

    def gather_pair(g):
        for i in ORDER if g == 0 else (5, 6, 4, 1, 2, 0):
            pass_on(g, 0, slots[i], sib).wait_recv()
            pass_on(g, 8 + i, slots[i], sib).start()

    def gather_end(g):
        for k in range(8):
            pass_on(g, 0, (1 - core) * 8 + k, sib).wait_recv()
        own_copy(g).wait()

    gather_start(0)

    common = jnp.int32(EXPERTS - 1)
    for e in range(EXPERTS - 2, -1, -1):
        common = jnp.where(counts_ref[e] == tokens, e, common)
    others = [(common + 1 + j) % EXPERTS for j in range(EXPERTS - 1)]
    ids, cmb = ids_ref[...], comb_ref[...]
    is_c = ids == common
    cc_row = jnp.sum(jnp.where(is_c, cmb, 0.0), 0, keepdims=True)
    co_row = jnp.sum(jnp.where(is_c, 0.0, cmb), 0, keepdims=True)
    id_row = jnp.sum(jnp.where(is_c, 0.0, ids.astype(F32)), 0, keepdims=True)
    which = lax.broadcasted_iota(jnp.int32, (128, tokens), 0)
    grid = jnp.where(which == 0, cc_row, jnp.where(which == 1, co_row, id_row))
    columns = grid.T
    for i in range(16):
        at = (i % 2) * 8 + i // 2
        meta[at * bl : (at + 1) * bl, :] = columns[i * bl : (i + 1) * bl, :]

    gather_pair(0)
    gather_end(0)
    gather_start(1)

    def pair_rows(buf, i):
        return jnp.concatenate([buf[2 * i].astype(F32), buf[2 * i + 1].astype(F32)], 0)

    def prep_x(i, carry):
        rows = pl.ds(pl.multiple_of(i * 2 * bl, 2 * bl), 2 * bl)
        oid = meta[rows, 2:3]
        xv = pair_rows(tbuf, i)
        xs[rows, :] = xv.astype(BF)
        for j, e in enumerate(others):
            xm[j, rows, :] = jnp.where(oid == e.astype(F32), xv, 0.0).astype(BF)
        return carry

    def prep_c(i, carry):
        rows = pl.ds(pl.multiple_of(i * 2 * bl, 2 * bl), 2 * bl)
        m = meta[rows, :]
        cc, co, oid = m[:, 0:1], m[:, 1:2], m[:, 2:3]
        cv = pair_rows(cbuf, i)
        ro = (co * cv).astype(BF).astype(F32)
        rgc[rows, :] = (cc * cv).astype(BF)
        rgo[rows, :] = ro.astype(BF)
        for j, e in enumerate(others):
            rgm[j, rows, :] = jnp.where(oid == e.astype(F32), ro, 0.0).astype(BF)
        for e in range(EXPERTS):
            hit = (oid == float(e)).astype(F32)
            mo[e, rows, :] = jnp.broadcast_to(hit, (2 * bl, fc)).astype(BF)
        cb[0, rows, :] = jnp.broadcast_to(cc, (2 * bl, 256))
        cb[1, rows, :] = jnp.broadcast_to(co, (2 * bl, 256))
        return carry

    lax.fori_loop(0, 8, prep_x, 0)
    for a in range(2):
        for e in range(EXPERTS):
            w_copy(a, e).wait()

    my = pl.ds(pl.multiple_of(yl * half, half), half)
    his = pl.ds(pl.multiple_of((1 - yl) * half, half), half)
    hh = (pl.ds(0, half), pl.ds(half, half))
    qq = (pl.ds(0, quart), pl.ds(quart, quart))
    mq = (
        pl.ds(pl.multiple_of(yl * half, quart), quart),
        pl.ds(pl.multiple_of(yl * half + quart, quart), quart),
    )
    gg = (pl.ds(0, 2), pl.ds(2, 1))

    def by(g, r):
        return sec(pb.at[r, gg[g], his], rby.at[r, gg[g]], b_send.at[g, r], b_recv.at[g, r], yp)

    def ar(g, d):
        return sec(
            pa.at[0, gg[g], hh[d]], rar.at[d, gg[g]], a_send.at[g, d], a_recv.at[g, d], zdev[d]
        )

    def af(g, d, h):
        i = 2 + 2 * d + h
        return sec(
            pa.at[1 + d, gg[g], hh[h]], raf.at[d, gg[g], hh[h]], a_send.at[g, i], a_recv.at[g, i],
            zdev[d],
        )

    def ay(g):
        return sec(sa.at[gg[g]], ray.at[gg[g]], a_send.at[g, 6], a_recv.at[g, 6], yp)

    def br(g, d):
        i = 4 + d
        return sec(
            qb.at[0, gg[g], qq[d]], rbr.at[d, gg[g]], b_send.at[g, i], b_recv.at[g, i], zdev[d]
        )

    def bf(g, d, h):
        i = 6 + 2 * d + h
        return sec(
            qb.at[1 + d, gg[g], qq[h]], rbf.at[d, gg[g], qq[h]], b_send.at[g, i], b_recv.at[g, i],
            zdev[d],
        )

    def chunk_of(r):
        zc = (z + 2 - r + 3 * (r // 2) - 2 * (r // 3)) % NZ
        return pl.ds(pl.multiple_of(zc * fc, fc), fc)

    def leave(g, r):
        @pl.when(r == 0)
        def _():
            ar(g, 0).start()
            ar(g, 1).start()

        @pl.when(r == 1)
        def _():
            af(g, 0, 1).start()

        @pl.when(r == 2)
        def _():
            af(g, 1, 0).start()

    def first_gu(r, carry):
        cols = chunk_of(r)

        @pl.when(r == 2)
        def _():
            gather_mid()

        def proj_c(a, c2):
            acc = mm(xs[...], wgu[a, common, :, cols])
            paf[r, a] = acc
            pa[r, a] = acc.astype(BF)
            return c2

        lax.fori_loop(0, 2, proj_c, 0)
        leave(0, r)

        def proj_o(a, c2):
            acc = mm(xm[0], wgu[a, others[0], :, cols])
            acc += mm(xm[1], wgu[a, others[1], :, cols])
            acc += mm(xm[2], wgu[a, others[2], :, cols])
            pbf[r, a] = acc
            pb[r, a] = acc.astype(BF)
            return c2

        lax.fori_loop(0, 2, proj_o, 0)
        by(0, r).start()
        return carry

    def first_dh(r, carry):
        cols = chunk_of(r)

        @pl.when(r == 2)
        def _():
            b_step(0, 1)

        acc = mm_nt(rgc[...], wd[common, cols, :])
        paf[r, 2] = acc
        pa[r, 2] = acc.astype(BF)
        leave(1, r)
        acc = mm_nt(rgm[0], wd[others[0], cols, :])
        acc += mm_nt(rgm[1], wd[others[1], cols, :])
        acc += mm_nt(rgm[2], wd[others[2], cols, :])
        pbf[r, 2] = acc
        pb[r, 2] = acc.astype(BF)
        by(1, r).start()
        return carry

    def a_relay(g):
        for d in (0, 1):
            ar(g, d).wait_recv()
            pa[1 + d, gg[g], hh[d]] = (
                paf[1 + d, gg[g], hh[d]] + rar[d, gg[g]].astype(F32)
            ).astype(BF)
            af(g, d, d).start()

    def a_final(g):
        for d in (0, 1):
            for h in (0, 1):
                af(g, d, h).wait_recv()
        sa[gg[g]] = (
            paf[3, gg[g], his]
            + raf[0, gg[g], his].astype(F32)
            + raf[1, gg[g], his].astype(F32)
        ).astype(BF)
        ay(g).start()

    def b_step(g, r):
        by(g, r).wait_recv()
        if r == 0:
            qb[0, gg[g]] = (pbf[0, gg[g], my] + rby[0, gg[g]].astype(F32)).astype(BF)
            br(g, 0).start()
            br(g, 1).start()
        elif r < 3:
            d = r - 1
            h = 1 - d
            qb[r, gg[g], qq[h]] = (
                pbf[r, gg[g], mq[h]] + rby[r, gg[g], qq[h]].astype(F32)
            ).astype(BF)
            bf(g, d, h).start()
            br(g, d).wait_recv()
            qb[r, gg[g], qq[d]] = (
                pbf[r, gg[g], mq[d]]
                + rby[r, gg[g], qq[d]].astype(F32)
                + rbr[d, gg[g]].astype(F32)
            ).astype(BF)
            bf(g, d, d).start()

    lax.fori_loop(0, NZ, first_gu, 0)
    gather_pair(1)
    a_relay(0)
    b_step(0, 0)
    gather_end(1)
    lax.fori_loop(0, 8, prep_c, 0)
    for e in range(EXPERTS):
        w_copy(2, e).wait()
    lax.fori_loop(0, NZ, first_dh, 0)
    b_step(0, 2)
    a_relay(1)
    a_final(0)
    b_step(0, 3)
    b_step(1, 0)
    b_step(1, 1)
    a_final(1)
    b_step(1, 2)
    b_step(1, 3)

    def swiglu(total, dst):
        gate, up, dh = total(0), total(1), total(2)
        sg = 1.0 / (1.0 + jnp.exp(-gate))
        act = gate * sg
        dst[z, 0, my, :] = (act * up).astype(BF)
        dst[z, 1, my, :] = (dh * up * sg * (1.0 + gate * (1.0 - sg))).astype(BF)
        dst[z, 2, my, :] = (dh * act).astype(BF)

    for g in (0, 1):
        for d in (0, 1):
            for h in (0, 1):
                bf(g, d, h).wait_recv()
    swiglu(
        lambda a: pbf[3, a, my, :]
        + rby[3, a].astype(F32)
        + rbf[0, a].astype(F32)
        + rbf[1, a].astype(F32),
        ho,
    )

    z1, z3, z2 = (z + 1) % NZ, (z + 3) % NZ, (z + 2) % NZ

    def oz(zc, d):
        return sec(ho.at[zc, :, my], ho.at[zc, :, my], o_send.at[d], o_recv.at[d], zdev[d])

    def oy(zc, i, rows):
        return sec(ho.at[zc, :, rows], ho.at[zc, :, rows], o_send.at[4 + i], o_recv.at[4 + i], yp)

    def orl(zc, d):
        part = ho.at[zc, :, mq[d]]
        return sec(part, part, o_send.at[2 + d], o_recv.at[2 + d], zdev[d])

    oz(z, 0).start()
    oz(z, 1).start()
    oy(z, 0, my).start()

    ay(0).wait_recv()
    ay(1).wait_recv()
    swiglu(
        lambda a: paf[3, a, my, :]
        + raf[0, a, my, :].astype(F32)
        + raf[1, a, my, :].astype(F32)
        + ray[a].astype(F32),
        hc,
    )

    def cy(rows):
        return sec(hc.at[z, :, rows], hc.at[z, :, rows], c_send.at[0], c_recv.at[0], yp)

    def cz(zc, h, rows, d):
        i = 1 + 2 * d + h
        return sec(hc.at[zc, :, rows], hc.at[zc, :, rows], c_send.at[i], c_recv.at[i], zdev[d])

    def crl(zc, d):
        part = hc.at[zc, :, hh[d]]
        return sec(part, part, c_send.at[5 + d], c_recv.at[5 + d], zdev[d])

    cy(my).start()
    cz(z, yl, my, 0).start()
    cz(z, yl, my, 1).start()

    oz(z3, 0).wait_recv()
    orl(z3, 0).start()
    oy(z3, 1, my).start()
    oz(z1, 1).wait_recv()
    orl(z1, 1).start()
    oy(z1, 2, my).start()
    cy(his).wait_recv()
    cz(z, 1 - yl, his, 0).start()
    cz(z, 1 - yl, his, 1).start()

    xf[...] = jnp.zeros_like(xf)
    cf[...] = jnp.zeros_like(cf)
    for g in (0, 1):
        for r in range(NZ):
            by(g, r).wait_send()

    mine = pl.ds(pl.multiple_of(core * half, half), half)
    theirs = pl.ds(pl.multiple_of((1 - core) * half, half), half)

    def tile(i):
        return pl.ds(pl.multiple_of(i * 256, 256), 256)

    def pair(i):
        return ten(fs.at[i], fr.at[i], p_send.at[i], p_recv.at[i], sib)

    def out_send(i, k):
        return ten(gs.at[i, k], gr.at[i, kt], f_send.at[i, k], f_recv.at[i, kt], k * 2 + core)

    def both(i, k):
        rows = pl.ds(pl.multiple_of(core * half + k * bl, 8), bl)
        return jnp.concatenate([xf[rows, tile(i)], cf[rows, tile(i)]], 0)

    def flush(i):
        pair(i).wait_recv()
        xf[mine, tile(i)] += fr[i, 0].astype(F32)
        cf[mine, tile(i)] += fr[i, 1].astype(F32)

        for d, flip in HOPS:
            k = ((x + d) % 4) * 2 + yh + flip - 2 * yh * flip
            gs[i, k] = both(i, k).astype(BF)
            out_send(i, k).start()

    def second(r, carry):
        zc = (z + 3 * r - 5 * (r // 2) - 2 * (r // 3)) % NZ
        cols = pl.ds(pl.multiple_of(zc * fc, fc), fc)

        @pl.when(r == 1)
        def _():
            for d in (0, 1):
                orl(z2, d).wait_recv()
            oy(z2, 3, my).start()
            cz(z3, 0, hh[0], 0).wait_recv()
            crl(z3, 0).start()
            cz(z1, 1, hh[1], 1).wait_recv()
            crl(z1, 1).start()
            cz(z3, 1, hh[1], 0).wait_recv()

        @pl.when(r == 2)
        def _():
            cz(z1, 0, hh[0], 1).wait_recv()

        @pl.when(r == 3)
        def _():
            crl(z2, 0).wait_recv()
            crl(z2, 1).wait_recv()

        def common_tile(i, c2):
            ns = tile(i)
            xf[:, ns] += cb[0] * mm(hc[zc, 0], wd[common, cols, ns])
            cf[:, ns] += mm_nt(hc[zc, 1], wgu[0, common, ns, cols]) + mm_nt(
                hc[zc, 2], wgu[1, common, ns, cols]
            )
            return c2

        lax.fori_loop(0, nt, common_tile, 0)

        @pl.when(r == 0)
        def _():
            oy(z, 0, his).wait_recv()

        @pl.when(r == 1)
        def _():
            oy(z3, 1, his).wait_recv()

        @pl.when(r == 2)
        def _():
            oy(z1, 2, his).wait_recv()

        @pl.when(r == 3)
        def _():
            oy(z2, 3, his).wait_recv()

        for j, e in enumerate(others):
            hit = mo[e]
            for a in range(3):
                pb[j, a] = ho[zc, a] * hit

        def other_tile(i, c2):
            ns = tile(i)
            acc = mm(pb[0, 0], wd[others[0], cols, ns])
            acc += mm(pb[1, 0], wd[others[1], cols, ns])
            acc += mm(pb[2, 0], wd[others[2], cols, ns])
            xf[:, ns] += cb[1] * acc
            acc = mm_nt(pb[0, 1], wgu[0, others[0], ns, cols])
            acc += mm_nt(pb[0, 2], wgu[1, others[0], ns, cols])
            for j in (1, 2):
                acc += mm_nt(pb[j, 1], wgu[0, others[j], ns, cols])
                acc += mm_nt(pb[j, 2], wgu[1, others[j], ns, cols])
            cf[:, ns] += acc

            @pl.when(r == 3)
            def _():
                fs[i, 0] = xf[theirs, ns].astype(BF)
                fs[i, 1] = cf[theirs, ns].astype(BF)
                pair(i).start()

            return c2

        lax.fori_loop(0, nt, other_tile, 0)
        return carry

    lax.fori_loop(0, NZ, second, 0)
    for i in range(nt):
        flush(i)

    def weight_grad(e, carry):
        here = (common == e).astype(F32)
        mc = here.astype(BF)
        hit = mo[e]
        xs[...] = rgc[...] * mc + rgo[...] * (1.0 - here).astype(BF)

        def block(zc, c2):
            hs = hc[zc, 0] * mc + ho[zc, 0] * hit
            rows = pl.ds(pl.multiple_of(zc * fc, fc), fc)
            for i in range(nt):
                ns = pl.ds(i * 256, 256)
                dd_ref[e, rows, ns] = mm_tn(hs, xs[:, ns]).astype(BF)
            return c2

        lax.fori_loop(0, NZ, block, 0)
        return carry

    lax.fori_loop(0, EXPERTS, weight_grad, 0)

    for i in range(nt):
        total = both(i, kt)
        for n in range(1, 8):
            k = (kt + n) % 8
            dev = k * 2 + core
            ten(gs.at[i, k], gr.at[i, k], f_send.at[i, k], f_recv.at[i, k], dev).wait_recv()
            total += gr[i, k].astype(F32)
        lo_ref[:, i * 256 : (i + 1) * 256] = total[:bl].astype(BF)
        dt_ref[:, i * 256 : (i + 1) * 256] = total[bl:].astype(BF)

    for i in range(nt):
        pair(i).wait_send()
        for n in range(1, 8):
            out_send(i, (kt + n) % 8).wait_send()
    for g in (0, 1):
        for i in range(8):
            if g == 0 or i > 2:
                own_send(g, i).wait_send()
            else:
                pass_on(g, i, slots[3], targets[4 + i]).wait_send()
        for i in range(7):
            pass_on(g, 8 + i, slots[i], sib).wait_send()
        for d in (0, 1):
            ar(g, d).wait_send()
            br(g, d).wait_send()
            for h in (0, 1):
                af(g, d, h).wait_send()
                bf(g, d, h).wait_send()
        ay(g).wait_send()
    for d, zc in ((0, z3), (1, z1)):
        oz(z, d).wait_send()
        orl(zc, d).wait_send()
        crl(zc, d).wait_send()
        cz(z, yl, my, d).wait_send()
        cz(z, 1 - yl, his, d).wait_send()
    for i, zc in enumerate((z, z3, z1, z2)):
        oy(zc, i, my).wait_send()
    cy(my).wait_send()


def on_device(tokens, combine, expert_ids, expert_counts, w_gate, w_up, w_down, cotangent):
    total = combine.shape[0]
    bl, dloc = tokens.shape
    floc = w_gate.shape[2]
    fc = floc // NZ
    half, quart = total // 2, total // 4
    nt = dloc // 256
    any_spec = pl.BlockSpec(memory_space=pl.ANY)
    vmem = pl.BlockSpec(memory_space=pltpu.VMEM)
    V = pltpu.VMEM
    dma = pltpu.SemaphoreType.DMA
    return pl.pallas_call(
        layer_kernel,
        out_shape=(V((bl, dloc), BF), V((bl, dloc), BF), V((EXPERTS, floc, dloc), BF)),
        in_specs=[pl.BlockSpec(memory_space=pltpu.SMEM)] + [vmem] * 4 + [any_spec] * 3,
        out_specs=(vmem, vmem, vmem),
        scratch_shapes=[
            V((2, EXPERTS, dloc, floc), BF),
            V((EXPERTS, floc, dloc), BF),
            V((16, bl, dloc), BF),
            V((16, bl, dloc), BF),
            V((total, 128), F32),
            V((total, dloc), F32),
            V((total, dloc), F32),
            V((total, dloc), BF),
            V((EXPERTS - 1, total, dloc), BF),
            V((total, dloc), BF),
            V((total, dloc), BF),
            V((EXPERTS - 1, total, dloc), BF),
            V((EXPERTS, total, fc), BF),
            V((2, total, 256), F32),
            V((NZ, 3, total, fc), BF),
            V((NZ, 3, total, fc), F32),
            V((NZ, 3, total, fc), BF),
            V((NZ, 3, total, fc), F32),
            V((2, 3, half, fc), BF),
            V((2, 3, total, fc), BF),
            V((3, half, fc), BF),
            V((3, half, fc), BF),
            V((NZ, 3, half, fc), BF),
            V((3, 3, half, fc), BF),
            V((2, 3, quart, fc), BF),
            V((2, 3, half, fc), BF),
            V((NZ, 3, total, fc), BF),
            V((NZ, 3, total, fc), BF),
            V((nt, 2, half, 256), BF),
            V((nt, 2, half, 256), BF),
            V((nt, 8, 2 * bl, 256), BF),
            V((nt, 8, 2 * bl, 256), BF),
            dma((3, EXPERTS)),
            dma((2,)),
            dma((2, 15)),
            dma((2, 16)),
            dma((2, 7)),
            dma((2, 7)),
            dma((2, 10)),
            dma((2, 10)),
            dma((7,)),
            dma((7,)),
            dma((8,)),
            dma((8,)),
            dma((nt,)),
            dma((nt,)),
            dma((nt, 8)),
            dma((nt, 8)),
        ],
        compiler_params=pltpu.CompilerParams(
            collective_id=0, has_side_effects=True, vmem_limit_bytes=VLIM
        ),
    )(expert_counts, combine.T, expert_ids.T, tokens, cotangent, w_gate, w_up, w_down)


def solution(mesh):
    in_specs = (
        P("tensor", "section"),
        P(),
        P(),
        P(),
        P(None, "section", "tensor"),
        P(None, "section", "tensor"),
        P(None, "tensor", "section"),
        P("tensor", "section"),
    )
    out_specs = (P("tensor", "section"), P("tensor", "section"), P(None, "tensor", "section"))
    return jax.shard_map(
        on_device, mesh=mesh, in_specs=in_specs, out_specs=out_specs, check_vma=False
    )
```
